256 devices in a mesh: section: 2 (over core), chan: 32 (over z, x), feed: 4 (over y).
Axes of the slice: x: 4, y: 4, z: 8, core: 2. Of those that a mesh axis runs over, the one named last changes fastest.
Arguments:
- voltages: bfloat16 [2, 1024, 24, 8192], P(None, 'feed', 'section', 'chan'), may hold values from -4 to 4
- positions: int32 [1024], replicated, may hold values from 0 to 1023, each once
- chan_delays: int32 [16, 8192], replicated, may hold values from 0 to 2
- sub_delays: int32 [256, 32], replicated, may hold values from 0 to 4
- boxcars: int32 [3, 2], replicated, may hold values from 1 to 6, as said below
Outputs:
- boxcar_snr: float32 [1024, 24, 3, 256], P(('chan', 'feed'), 'section')
The draws below stay inside these ranges and needn't reach their ends.
Inputs may be any that keep to these rules, and one draw needn't show every extreme that they name: `boxcars`: column 0 holds the widths 2 to 4, each once; column 1 holds dilations of 1 or more with (width - 1) * dilation <= 6; the filter of width 2 has dilation 6 and the widest filter dilation 1.
All inputs are finite; a program needn't handle non-finite values.
Results may differ from the reference program's by a relative error of at most 0.0033.
Values may be sent and summed in bfloat16 or wider, within the bound.
A program may use at most 64 MiB of HBM per device.

```python
import math
import jax
import jax.numpy as jnp
from jax import lax

NF = 1024
C = 8192
NSB = 32
NK = 16
ND = 256
NW = 3
D1MAX = 2
D2MAX = 4
BOXMAX = 6
TT = 24
SUBCH = 256
RIM = 12


def draw_voltages(key, part):
    gain_key = jax.random.fold_in(key, 11)
    feed_key = jax.random.fold_in(key, 12)
    base_key = jax.random.fold_in(key, 13)
    chan_gain = jnp.exp(jax.random.uniform(gain_key, (C,), jnp.float32, 0.0, math.log(10.0)))
    feed_gain = jnp.exp(jax.random.uniform(feed_key, (NF,), jnp.float32, -math.log(2.0), math.log(2.0)))
    base_draw = jnp.clip(jax.random.normal(base_key, (2, NF, TT, C), jnp.float32), -6.0, 6.0)
    scaled = base_draw * chan_gain[None, None, None, :] * feed_gain[None, :, None, None]
    return jnp.clip(scaled / math.sqrt(NF), -4.0, 4.0).astype(jnp.bfloat16)


def draw_chan_delays(key, part):
    value_key = jax.random.fold_in(key, 21)
    place_key = jax.random.fold_in(key, 22)
    delays = jax.random.randint(value_key, (NK, C), 0, D1MAX + 1, dtype=jnp.int32)
    places = jax.random.randint(place_key, (NK, 1), 0, C, dtype=jnp.int32)
    columns = jnp.arange(C, dtype=jnp.int32)[None, :]
    return jnp.where(columns == places, D1MAX, delays).astype(jnp.int32)


def draw_sub_delays(key, part):
    value_key = jax.random.fold_in(key, 31)
    place_key = jax.random.fold_in(key, 32)
    delays = jax.random.randint(value_key, (ND, NSB), 0, D2MAX + 1, dtype=jnp.int32)
    places = jax.random.randint(place_key, (ND, 1), 0, NSB, dtype=jnp.int32)
    columns = jnp.arange(NSB, dtype=jnp.int32)[None, :]
    return jnp.where(columns == places, D2MAX, delays).astype(jnp.int32)


def draw_boxcars(key, part):
    order_key = jax.random.fold_in(key, 41)
    reach_key = jax.random.fold_in(key, 42)
    widths = (2 + jax.random.permutation(order_key, NW)).astype(jnp.int32)
    longest = BOXMAX // (widths - 1)
    dilations = jax.random.randint(reach_key, (NW,), 1, longest + 1, dtype=jnp.int32)
    dilations = jnp.where(widths == 2, longest, dilations)
    dilations = jnp.where(widths == NW + 1, 1, dilations)
    return jnp.stack([widths, dilations], axis=1).astype(jnp.int32)


def setup_inputs(seed: int = 0) -> dict:
    key_of = jax.random.split(jax.random.key(seed), 6)
    voltages = draw_voltages(jax.random.fold_in(key_of[5], 71), 0)
    positions = jax.random.permutation(key_of[1], NF).astype(jnp.int32)
    chan_delays = draw_chan_delays(jax.random.fold_in(key_of[5], 71), 0)
    sub_delays = draw_sub_delays(jax.random.fold_in(key_of[5], 71), 0)
    boxcars = draw_boxcars(jax.random.fold_in(key_of[5], 71), 0)
    return {"voltages": voltages, "positions": positions, "chan_delays": chan_delays, "sub_delays": sub_delays, "boxcars": boxcars}


EPSILON = 1e-05

def phase_matrix(positions):
    beam_ids = jnp.arange(NF, dtype=jnp.int32)
    phase_ids = beam_ids[:, None] * positions[None, :] % NF
    angles = phase_ids.astype(jnp.float32) * (2.0 * math.pi / NF)
    cosine = jnp.cos(angles)
    sine = jnp.sin(angles)
    upper = jnp.concatenate([cosine, sine], axis=1)
    lower = jnp.concatenate([-sine, cosine], axis=1)
    return jnp.concatenate([upper, lower], axis=0).astype(jnp.bfloat16)

def delay_selectors(delays, largest):
    return jnp.stack([(delays == value).astype(jnp.float32) for value in range(largest + 1)])

def section_one(extended, selectors, segment_size, span_len):
    row_count = extended.shape[0]
    extent = extended.shape[2]
    segment_count = extent // segment_size
    summed = None
    for offset in range(selectors.shape[0]):
        window_part = extended[:, offset:offset + span_len, :].reshape(row_count, span_len, segment_count, segment_size)
        chooser = selectors[offset].reshape(selectors.shape[1], segment_count, segment_size)
        partial_value = jnp.einsum('btnc,knc->btnk', window_part, chooser, precision=lax.Precision.HIGHEST)
        summed = partial_value if summed is None else summed + partial_value
    return summed

def section_two(subband, sub_delays, span_len):
    row_count = subband.shape[0]
    band_count = subband.shape[2]
    trials_k = subband.shape[3]
    flat = subband.reshape(row_count, subband.shape[1], band_count * trials_k)
    trial_ids = jnp.arange(ND, dtype=jnp.int32)
    chosen = jnp.arange(NK, dtype=jnp.int32)[:, None] == (trial_ids * NK // ND)[None, :]
    summed = None
    for offset in range(D2MAX + 1):
        matches = jnp.transpose(sub_delays) == offset
        weights = (matches[:, None, :] & chosen[None, :, :]).astype(jnp.float32).reshape(band_count * trials_k, ND)
        partial_value = jnp.einsum('btj,jm->btm', flat[:, offset:offset + span_len, :], weights, precision=lax.Precision.HIGHEST)
        summed = partial_value if summed is None else summed + partial_value
    return summed * (1.0 / math.sqrt(C))

def boxcar_filter(dedispersed, boxcars, span_len):
    outputs = []
    for filter_index in range(NW):
        width_now = boxcars[filter_index, 0]
        stride_now = boxcars[filter_index, 1]
        summed = jnp.zeros((dedispersed.shape[0], span_len, dedispersed.shape[2]), jnp.float32)
        for offset in range(NW + 1):
            window_part = lax.dynamic_slice_in_dim(dedispersed, offset * stride_now, span_len, 1)
            summed = summed + jnp.where(offset < width_now, window_part, 0.0)
        outputs.append(summed * lax.rsqrt(width_now.astype(jnp.float32)))
    return jnp.stack(outputs, axis=2)

def reference(voltages, positions, chan_delays, sub_delays, boxcars):
    phases_table = phase_matrix(positions)
    span_sub = TT + D2MAX + BOXMAX

    def subband_block(index):
        start = index * SUBCH
        block = lax.dynamic_slice_in_dim(voltages, start, SUBCH, 3)
        flat = block.reshape(2 * NF, TT * SUBCH)
        product = jnp.dot(phases_table, flat, preferred_element_type=jnp.float32)
        real_part = product[:NF]
        imag_part = product[NF:]
        beam_power = (real_part * real_part + imag_part * imag_part).reshape(NF, TT, SUBCH)
        baseline_level = lax.optimization_barrier(jnp.sum(beam_power, axis=1)) / TT
        normed = beam_power / (baseline_level[:, None, :] + EPSILON) - 1.0
        padded = jnp.pad(normed, ((0, 0), (0, RIM), (0, 0)))
        delays = lax.dynamic_slice_in_dim(chan_delays, start, SUBCH, 1)
        selectors = delay_selectors(delays, D1MAX)
        return section_one(padded, selectors, SUBCH, span_sub)[:, :, 0, :]
    outcome = lax.map(subband_block, jnp.arange(NSB, dtype=jnp.int32))
    subband = jnp.transpose(outcome, (1, 2, 0, 3))
    dedispersed = section_two(subband, sub_delays, TT + BOXMAX)
    return boxcar_filter(dedispersed, boxcars, TT)
```

```python
import math

import jax
import jax.numpy as jnp
from jax import lax
from jax.sharding import PartitionSpec as P

NF = 1024
C = 8192
NK = 16
ND = 256
NW = 3
D1MAX = 2
D2MAX = 4
BOXMAX = 6
SUBCH = 256
EPSILON = 1e-05


def beam_order(positions):
    chan = jnp.arange(32, dtype=jnp.int32)[None, :, None]
    feed = jnp.arange(4, dtype=jnp.int32)[:, None, None]
    low = jnp.arange(8, dtype=jnp.int32)[None, None, :]
    beam_ids = (chan * 32 + feed * 8 + low).reshape(NF)
    phase_ids = beam_ids[:, None] * positions[None, :] % NF
    angles = phase_ids.astype(jnp.float32) * (2.0 * math.pi / NF)
    cosine = jnp.cos(angles)
    sine = jnp.sin(angles)
    upper = jnp.concatenate([cosine, sine], axis=1)
    lower = jnp.concatenate([-sine, cosine], axis=1)
    return jnp.concatenate([upper, lower], axis=0).astype(jnp.bfloat16)


def two_part_dot(values, zero_one):
    high = values.astype(jnp.bfloat16)
    low = (values - high.astype(jnp.float32)).astype(jnp.bfloat16)
    first = jnp.dot(high, zero_one, preferred_element_type=jnp.float32)
    return first + jnp.dot(low, zero_one, preferred_element_type=jnp.float32)


def channel_selector(delays, span_t):
    local = delays.shape[1]
    times = jnp.arange(span_t, dtype=jnp.int32)[:, None, None, None]
    outs = jnp.arange(span_t + D1MAX, dtype=jnp.int32)[None, None, :, None]
    chosen = (times + D1MAX - outs) == jnp.transpose(delays)[None, :, None, :]
    return chosen.astype(jnp.bfloat16).reshape(span_t * local, (span_t + D1MAX) * NK)


def subband_selector(sub_delays):
    offsets = jnp.arange(D2MAX + 1, dtype=jnp.int32)[:, None, None, None]
    matches = jnp.transpose(sub_delays)[None, :, None, :] == offsets
    trial_k = jnp.arange(ND, dtype=jnp.int32) * NK // ND
    own = jnp.arange(NK, dtype=jnp.int32)[:, None] == trial_k[None, :]
    weights = matches & own[None, None, :, :]
    return weights.astype(jnp.bfloat16).reshape(D2MAX + 1, -1, ND)


def boxcar_filter(extended, boxcars, span_t):
    outputs = []
    for filter_index in range(NW):
        width_now = boxcars[filter_index, 0]
        stride_now = boxcars[filter_index, 1]
        summed = extended[:, :span_t]
        for offset in range(1, NW + 1):
            start = jnp.minimum(offset * stride_now, BOXMAX)
            window_part = lax.dynamic_slice_in_dim(extended, start, span_t, 1)
            summed = summed + jnp.where(offset < width_now, window_part, 0.0)
        outputs.append(summed * lax.rsqrt(width_now.astype(jnp.float32)))
    return jnp.stack(outputs, axis=2)


def per_device(voltages, positions, chan_delays, sub_delays, boxcars):
    gathered = lax.all_to_all(voltages, "feed", split_axis=3, concat_axis=1, tiled=True)
    span_t = gathered.shape[2]
    local = gathered.shape[3]
    table = beam_order(positions)
    flat = gathered.reshape(2 * NF, span_t * local)
    product = jnp.dot(table, flat, preferred_element_type=jnp.float32)
    real_part = product[:NF]
    imag_part = product[NF:]
    power = (real_part * real_part + imag_part * imag_part).reshape(NF, span_t, local)
    section_count = lax.axis_size("section")
    totals = lax.psum(jnp.sum(power, axis=1), "section")
    level = totals / (span_t * section_count)
    normed = power / (level[:, None, :] + EPSILON) - 1.0
    start = lax.axis_index("chan") * SUBCH + lax.axis_index("feed") * local
    delays = lax.dynamic_slice_in_dim(chan_delays, start, local, 1)
    partial = two_part_dot(normed.reshape(NF, span_t * local), channel_selector(delays, span_t))
    summed = lax.psum_scatter(partial, "feed", scatter_dimension=0, tiled=True)
    span_u = span_t + D1MAX
    blocks = summed.reshape(lax.axis_size("chan"), -1, span_u * NK)
    turned = lax.all_to_all(blocks, "chan", split_axis=0, concat_axis=0, tiled=True)
    bands, beams = turned.shape[0], turned.shape[1]
    subband = jnp.transpose(turned.reshape(bands, beams, span_u, NK), (1, 2, 0, 3))
    padded = jnp.pad(subband.reshape(beams, span_u, bands * NK), ((0, 0), (D2MAX, D2MAX), (0, 0)))
    span_v = span_u + D2MAX
    shifted = jnp.concatenate([padded[:, d : d + span_v] for d in range(D2MAX + 1)], axis=2)
    weights = subband_selector(sub_delays).reshape(-1, ND)
    dedispersed = two_part_dot(shifted.reshape(beams * span_v, -1), weights) * (1.0 / math.sqrt(C))
    dedispersed = dedispersed.reshape(beams, span_v, ND)
    later = lax.ppermute(dedispersed[:, :span_t], "section", [(1, 0)])
    extended = jnp.pad(dedispersed[:, BOXMAX:], ((0, 0), (0, BOXMAX), (0, 0)))
    extended = extended + jnp.pad(later, ((0, 0), (BOXMAX, 0), (0, 0)))
    return boxcar_filter(extended, boxcars, span_t)


def solution(mesh):
    return jax.shard_map(
        per_device,
        mesh=mesh,
        in_specs=(P(None, "feed", "section", "chan"), P(), P(), P(), P()),
        out_specs=P(("chan", "feed"), "section", None, None),
        check_vma=False,
    )
```

```python
import math

import jax
import jax.numpy as jnp
from jax import lax
from jax.experimental import pallas as pl
from jax.experimental.pallas import tpu as pltpu
from jax.sharding import PartitionSpec as P

NF = 1024
C = 8192
NK = 16
ND = 256
NW = 3
D1MAX = 2
D2MAX = 4
BOXMAX = 6
TT = 24
SUBCH = 256
EPSILON = 1e-05

SPAN = 12
LOCAL = 64
CHANS = 32
FEEDS = 4
CHUNKS = 3
SPAN_V = SPAN + BOXMAX
F32 = jnp.float32
BF16 = jnp.bfloat16
MESH = pl.DeviceIdType.MESH


def lane_ids(shape):
    return lax.broadcasted_iota(jnp.int32, shape, len(shape) - 1)


def row_ids(shape):
    return lax.broadcasted_iota(jnp.int32, shape, len(shape) - 2)


def kernel(
    v_ref, pos_ref, cd_ref, sd_ref, out_ref,
    vbuf, packed, arrived, relay_up, relay_down, table, acc, power,
    base_own, base_other, cdbuf, delay_t, chooser, weights,
    part_send, part_recv, block_send, block_recv, lhs, swap_send, swap_recv, trig,
    v_sem, cd_sem, a_send, a_recv, b_send, b_recv, p_send, p_recv, q_send, q_recv, s_send, s_recv,
):
    sec = lax.axis_index("section")
    ch = lax.axis_index("chan")
    fd = lax.axis_index("feed")
    up, down, far = lax.rem(fd + 1, 4), lax.rem(fd + 3, 4), lax.rem(fd + 2, 4)

    loads = []
    for j in range(CHUNKS):
        loads.append(
            pltpu.make_async_copy(v_ref.at[:, pl.ds(4 * j, 4)], vbuf.at[:, pl.ds(4 * j, 4)], v_sem.at[j])
        )
        loads[j].start()
    first = pl.multiple_of(ch * SUBCH, SUBCH)
    cd_load = pltpu.make_async_copy(cd_ref.at[:, pl.ds(first, SUBCH)], cdbuf, cd_sem)
    cd_load.start()

    barrier = pltpu.get_barrier_semaphore()
    for other in (up, down, far):
        pl.semaphore_signal(barrier, inc=1, device_id={"feed": other}, device_id_type=MESH)
    pl.semaphore_signal(barrier, inc=1, device_id={"section": 1 - sec}, device_id_type=MESH)

    @pl.loop(1, CHANS)
    def _(i):
        pl.semaphore_signal(
            barrier, inc=1, device_id={"chan": lax.rem(ch + i, CHANS)}, device_id_type=MESH
        )

    low_half = lane_ids((256, 128)) < LOCAL
    for j in range(CHUNKS):
        loads[j].wait()
        for part in range(2):
            for pair in range(2):
                for tile in range(2):
                    lanes = pl.ds(128 * tile, 128)
                    a = vbuf[part, 4 * j + 2 * pair, :, lanes]
                    b = vbuf[part, 4 * j + 2 * pair + 1, :, lanes]
                    even = jnp.where(low_half, a, pltpu.roll(b, LOCAL, 1))
                    odd = jnp.where(low_half, pltpu.roll(a, LOCAL, 1), b)
                    rows = pl.ds(256 * part, 256)
                    packed[2 * tile, j, rows, pl.ds(128 * pair, 128)] = even
                    packed[2 * tile + 1, j, rows, pl.ds(128 * pair, 128)] = odd

    pl.semaphore_wait(barrier, 3 + 1 + CHANS - 1)

    def to_feed(src, dst, sems, index, other):
        copy = pltpu.make_async_remote_copy(
            src_ref=src, dst_ref=dst, send_sem=sems[0].at[index], recv_sem=sems[1].at[index],
            device_id={"feed": other}, device_id_type=MESH,
        )
        copy.start()
        return copy

    a_sems = (a_send, a_recv)
    halves_up, halves_down, direct_up, direct_down, passed_up, passed_down = [], [], [], [], [], []
    re_rows, im_rows = pl.ds(0, 256), pl.ds(256, 256)
    for j in range(CHUNKS):
        halves_up.append(to_feed(packed.at[far, j, re_rows], relay_up.at[j], a_sems, 6 * j, up))
        halves_down.append(to_feed(packed.at[far, j, im_rows], relay_down.at[j], a_sems, 6 * j + 1, down))
    for j in range(CHUNKS):
        direct_up.append(to_feed(packed.at[up, j], arrived.at[j, 0], a_sems, 6 * j + 2, up))
        direct_down.append(to_feed(packed.at[down, j], arrived.at[j, 1], a_sems, 6 * j + 3, down))

    step = 2.0 * math.pi / NF
    for q, owner in enumerate((fd, down, up, far)):
        place = jnp.concatenate(
            [pos_ref[pl.ds(2 * owner, 1), :], pos_ref[pl.ds(2 * owner + 1, 1), :]], axis=1
        )
        ids = row_ids((32, 256))
        fine = ((ids * place) & (NF - 1)).astype(F32) * step
        coarse = ((ids * 32 * place) & (NF - 1)).astype(F32) * step
        trig[0] = jnp.cos(coarse)
        trig[1] = jnp.sin(coarse)
        trig[2] = jnp.cos(fine)
        trig[3] = jnp.sin(fine)

        @pl.loop(0, CHANS // 2)
        def _(i):
            cos_c = jnp.concatenate(
                [jnp.broadcast_to(trig[0, pl.ds(2 * i + n, 1), :], (8, 256)) for n in range(2)], axis=0
            )
            sin_c = jnp.concatenate(
                [jnp.broadcast_to(trig[1, pl.ds(2 * i + n, 1), :], (8, 256)) for n in range(2)], axis=0
            )
            for f in range(FEEDS):
                cos_f = jnp.concatenate([trig[2, 8 * f : 8 * f + 8, :]] * 2, axis=0)
                sin_f = jnp.concatenate([trig[3, 8 * f : 8 * f + 8, :]] * 2, axis=0)
                cosine = (cos_c * cos_f - sin_c * sin_f).astype(BF16)
                sine = sin_c * cos_f + cos_c * sin_f
                upper = pl.ds(pl.multiple_of(256 * f + 16 * i, 16), 16)
                lower = pl.ds(pl.multiple_of(NF + 256 * f + 16 * i, 16), 16)
                table[q, upper, 0:256] = cosine
                table[q, upper, 256:512] = sine.astype(BF16)
                table[q, lower, 0:256] = (-sine).astype(BF16)
                table[q, lower, 256:512] = cosine

    def block_dot(q, rows, right):
        return jnp.dot(table[q, rows, :], right, preferred_element_type=F32)

    for j in range(CHUNKS):
        @pl.loop(0, 4)
        def _(m):
            rows = pl.ds(pl.multiple_of(512 * m, 512), 512)
            acc[j, rows, :] = block_dot(0, rows, packed[fd, j])

    for j in range(CHUNKS):
        halves_up[j].wait_recv()
        passed_up.append(to_feed(relay_up.at[j], arrived.at[j, 2, re_rows], a_sems, 6 * j + 4, up))
        halves_down[j].wait_recv()
        passed_down.append(to_feed(relay_down.at[j], arrived.at[j, 2, im_rows], a_sems, 6 * j + 5, down))

    cd_load.wait()
    one_k = (row_ids((NK, 256)) == (lane_ids((NK, 256)) & (NK - 1))).astype(BF16)
    delay_t[...] = lax.dot_general(
        cdbuf[...].astype(F32).astype(BF16), one_k, (((0,), (0,)), ((), ())), preferred_element_type=F32
    )
    mine = delay_t[pl.ds(pl.multiple_of(fd * LOCAL, LOCAL), LOCAL), :]
    lanes = lane_ids((LOCAL, 256))
    turned = (lanes & 128) // 16 + (((lanes & 127) // 16 + 8 - lax.rem(ch, 8)) & 7)
    turned = turned.astype(F32)
    for t in range(SPAN):
        hit = (turned + mine) == float(t + D1MAX)
        chooser[LOCAL * t : LOCAL * (t + 1), :] = jnp.where(hit, 1.0, 0.0).astype(BF16)

    own_k = row_ids((NK, ND)) == lane_ids((NK, ND)) * NK // ND

    @pl.loop(0, CHANS)
    def _(s):
        delay = jnp.broadcast_to(sd_ref[pl.ds(s, 1), :], (NK, ND))
        rows = pl.ds(pl.multiple_of(NK * s, NK), NK)
        for d in range(D2MAX + 1):
            weights[d, rows, :] = jnp.where(own_k & (delay == d), 1.0, 0.0).astype(BF16)

    for j in range(CHUNKS):
        direct_up[j].wait_recv()
        direct_down[j].wait_recv()

        @pl.loop(0, 4)
        def _(m):
            rows = pl.ds(pl.multiple_of(512 * m, 512), 512)
            acc[j, rows, :] += block_dot(1, rows, arrived[j, 0]) + block_dot(2, rows, arrived[j, 1])

    def beam_power(j, f):
        rows = pl.ds(pl.multiple_of(256 * f, 256), 256)
        lower = pl.ds(pl.multiple_of(NF + 256 * f, 256), 256)
        right = arrived[j, 2]
        re = acc[j, rows, :] + block_dot(3, rows, right)
        im = acc[j, lower, :] + block_dot(3, lower, right)
        power[rows, 256 * j : 256 * (j + 1)] = re * re + im * im

    for j in range(CHUNKS):
        passed_up[j].wait_recv()
        passed_down[j].wait_recv()
        if j < CHUNKS - 1:
            @pl.loop(0, FEEDS)
            def _(f):
                beam_power(j, f)

    order = (far, up, down, fd)
    base_copies = []
    for n, f in enumerate(order):
        beam_power(CHUNKS - 1, f)
        rows = pl.ds(pl.multiple_of(256 * f, 256), 256)
        total = power[rows, 0:128]
        for tile in range(1, 6):
            total = total + power[rows, 128 * tile : 128 * (tile + 1)]
        base_own[n] = total + pltpu.roll(total, LOCAL, 1)
        copy = pltpu.make_async_remote_copy(
            src_ref=base_own.at[n], dst_ref=base_other.at[n], send_sem=b_send.at[n], recv_sem=b_recv.at[n],
            device_id={"section": 1 - sec}, device_id_type=MESH,
        )
        copy.start()
        base_copies.append(copy)

    part_copies = []
    own = None
    for n, f in enumerate(order):
        base_copies[n].wait_recv()
        rows = pl.ds(pl.multiple_of(256 * f, 256), 256)
        scale = 1.0 / ((base_own[n] + base_other[n]) * (1.0 / TT) + EPSILON)
        summed = None
        for tile in range(3):
            normed = jnp.concatenate(
                [power[rows, 256 * tile + 128 * h : 256 * tile + 128 * (h + 1)] * scale - 1.0 for h in range(2)],
                axis=1,
            )
            high = normed.astype(BF16)
            low = (normed - high.astype(F32)).astype(BF16)
            chosen = chooser[256 * tile : 256 * (tile + 1), :]
            term = jnp.dot(high, chosen, preferred_element_type=F32) + jnp.dot(
                low, chosen, preferred_element_type=F32
            )
            summed = term if summed is None else summed + term
        blocks = jnp.concatenate(
            [summed[:, 0:128].reshape(CHANS, 8, 128), summed[:, 128:256].reshape(CHANS, 8, 128)], axis=1
        )
        if n < 3:
            part_send[n] = blocks.astype(BF16)
            part_copies.append(to_feed(part_send.at[n], part_recv.at[n], (p_send, p_recv), n, f))
        else:
            own = blocks
    for copy in part_copies:
        copy.wait_recv()
    for n in range(3):
        own = own + part_recv[n].astype(F32)
    block_send[...] = own.astype(BF16)

    def chan_copy(i):
        other = lax.rem(ch + i, CHANS)
        return pltpu.make_async_remote_copy(
            src_ref=block_send.at[other], dst_ref=block_recv.at[ch],
            send_sem=q_send.at[other], recv_sem=q_recv.at[ch],
            device_id={"chan": other}, device_id_type=MESH,
        )

    @pl.loop(1, CHANS)
    def _(i):
        chan_copy(i).start()

    block_recv[ch] = block_send[ch]
    lhs[0:32, :] = jnp.zeros((32, 512), F32)
    lhs[144:176, :] = jnp.zeros((32, 512), F32)

    @pl.loop(1, CHANS)
    def _(i):
        other = lax.rem(ch + i, CHANS)
        pltpu.make_async_remote_copy(
            src_ref=block_send.at[other], dst_ref=block_recv.at[other],
            send_sem=q_send.at[other], recv_sem=q_recv.at[other],
            device_id={"chan": other}, device_id_type=MESH,
        ).wait_recv()

    spot = lane_ids((8, 128)) // 16
    for g in range(4):
        wide = [block_recv[8 * g + s].astype(F32) for s in range(8)]
        for u in range(SPAN + D1MAX):
            h = u // 8
            mixed = wide[0][8 * h : 8 * h + 8]
            for s in range(1, 8):
                mixed = jnp.where(spot == (u + s) % 8, wide[s][8 * h : 8 * h + 8], mixed)
            shift = (128 - 16 * (u % 8)) % 128
            if shift:
                mixed = pltpu.roll(mixed, shift, 1)
            lhs[32 + 8 * u : 40 + 8 * u, 128 * g : 128 * (g + 1)] = mixed

    found = None
    for d in range(D2MAX + 1):
        term = jnp.dot(lhs[8 * d : 8 * d + 8 * SPAN_V, :].astype(BF16), weights[d], preferred_element_type=F32)
        found = term if found is None else found + term
    found = found * (1.0 / math.sqrt(C))
    swap_send[...] = found[0 : 8 * SPAN]
    swap = pltpu.make_async_remote_copy(
        src_ref=swap_send, dst_ref=swap_recv, send_sem=s_send, recv_sem=s_recv,
        device_id={"section": 1 - sec}, device_id_type=MESH,
    )
    swap.start()
    out_ref[0 : 8 * SPAN, :] = found[8 * BOXMAX : 8 * SPAN_V]
    out_ref[8 * SPAN : 8 * SPAN_V, :] = jnp.zeros((8 * BOXMAX, ND), F32)
    swap.wait_recv()
    taken = jnp.where(jnp.full((8 * SPAN, ND), sec, jnp.int32) == 0, swap_recv[...], 0.0)
    out_ref[8 * BOXMAX : 8 * SPAN_V, :] += taken

    for group in (halves_up, halves_down, direct_up, direct_down, passed_up, passed_down):
        for copy in group:
            copy.wait_send()
    for copy in base_copies + part_copies:
        copy.wait_send()

    @pl.loop(1, CHANS)
    def _(i):
        chan_copy(i).wait_send()

    swap.wait_send()


def search(voltages, positions, chan_delays, sub_delays):
    vmem, anywhere = pl.BlockSpec(memory_space=pltpu.VMEM), pl.BlockSpec(memory_space=pl.ANY)
    dma = pltpu.SemaphoreType.DMA
    return pl.pallas_call(
        kernel,
        out_shape=jax.ShapeDtypeStruct((8 * SPAN_V, ND), F32),
        in_specs=[anywhere, vmem, anywhere, vmem],
        out_specs=vmem,
        scratch_shapes=[
            pltpu.VMEM((2, SPAN, 256, 256), BF16),
            pltpu.VMEM((4, CHUNKS, 512, 256), BF16),
            pltpu.VMEM((CHUNKS, 3, 512, 256), BF16),
            pltpu.VMEM((CHUNKS, 256, 256), BF16),
            pltpu.VMEM((CHUNKS, 256, 256), BF16),
            pltpu.VMEM((4, 2 * NF, 512), BF16),
            pltpu.VMEM((CHUNKS, 2 * NF, 256), F32),
            pltpu.VMEM((NF, SPAN * LOCAL), F32),
            pltpu.VMEM((4, 256, 128), F32),
            pltpu.VMEM((4, 256, 128), F32),
            pltpu.VMEM((NK, SUBCH), jnp.int32),
            pltpu.VMEM((SUBCH, 256), F32),
            pltpu.VMEM((SPAN * LOCAL, 256), BF16),
            pltpu.VMEM((D2MAX + 1, 512, ND), BF16),
            pltpu.VMEM((3, CHANS, 16, 128), BF16),
            pltpu.VMEM((3, CHANS, 16, 128), BF16),
            pltpu.VMEM((CHANS, 16, 128), BF16),
            pltpu.VMEM((CHANS, 16, 128), BF16),
            pltpu.VMEM((176, 512), F32),
            pltpu.VMEM((8 * SPAN, ND), F32),
            pltpu.VMEM((8 * SPAN, ND), F32),
            pltpu.VMEM((4, 32, 256), F32),
            dma((CHUNKS,)),
            dma,
            dma((6 * CHUNKS,)),
            dma((6 * CHUNKS,)),
            dma((4,)),
            dma((4,)),
            dma((3,)),
            dma((3,)),
            dma((CHANS,)),
            dma((CHANS,)),
            dma,
            dma,
        ],
        compiler_params=pltpu.CompilerParams(
            collective_id=0, has_side_effects=True, vmem_limit_bytes=60 * 1024 * 1024
        ),
        name="search",
    )(
        jnp.transpose(voltages, (0, 2, 1, 3)),
        positions.reshape(8, 128),
        chan_delays,
        jnp.transpose(sub_delays),
    )


def boxcar_filter(extended, boxcars):
    outputs = []
    for filter_index in range(NW):
        width_now = boxcars[filter_index, 0]
        stride_now = boxcars[filter_index, 1]
        summed = extended[:SPAN]
        for offset in range(1, NW + 1):
            start = jnp.minimum(offset * stride_now, BOXMAX)
            window_part = lax.dynamic_slice_in_dim(extended, start, SPAN, 0)
            summed = summed + jnp.where(offset < width_now, window_part, 0.0)
        outputs.append(summed * lax.rsqrt(width_now.astype(F32)))
    return jnp.transpose(jnp.stack(outputs, axis=1), (2, 0, 1, 3))


def per_device(voltages, positions, chan_delays, sub_delays, boxcars):
    extended = search(voltages, positions, chan_delays, sub_delays)
    return boxcar_filter(extended.reshape(SPAN_V, 8, ND), boxcars)


def solution(mesh):
    return jax.shard_map(
        per_device,
        mesh=mesh,
        in_specs=(P(None, "feed", "section", "chan"), P(), P(), P(), P()),
        out_specs=P(("chan", "feed"), "section", None, None),
        check_vma=False,
    )
```

```python
import math

import jax
import jax.numpy as jnp
from jax import lax
from jax.experimental import pallas as pl
from jax.experimental.pallas import tpu as pltpu
from jax.sharding import PartitionSpec as P

NF = 1024
C = 8192
NK = 16
ND = 256
NW = 3
D1MAX = 2
D2MAX = 4
BOXMAX = 6
TT = 24
SUBCH = 256
EPSILON = 1e-05

SPAN = 12
LOCAL = 64
CHANS = 32
FEEDS = 4
CHUNKS = 3
SPAN_V = SPAN + BOXMAX
F32 = jnp.float32
BF16 = jnp.bfloat16
MESH = pl.DeviceIdType.MESH


def lane_ids(shape):
    return lax.broadcasted_iota(jnp.int32, shape, len(shape) - 1)


def row_ids(shape):
    return lax.broadcasted_iota(jnp.int32, shape, len(shape) - 2)


def kernel(
    v_ref, pos_ref, cd_ref, sd_ref, out_ref,
    vbuf, packed, arrived, relay_up, relay_down, table, acc, power,
    base_own, base_other, cdbuf, delay_t, chooser, weights,
    part_send, part_recv, block_send, block_recv, lhs, swap_send, swap_recv, trig,
    v_sem, cd_sem, a_send, a_recv, b_send, b_recv, p_send, p_recv, q_send, q_recv, s_send, s_recv,
):
    sec = lax.axis_index("section")
    ch = lax.axis_index("chan")
    fd = lax.axis_index("feed")
    up, down, far = lax.rem(fd + 1, 4), lax.rem(fd + 3, 4), lax.rem(fd + 2, 4)

    loads = []
    for j in range(CHUNKS):
        loads.append(
            pltpu.make_async_copy(v_ref.at[:, pl.ds(4 * j, 4)], vbuf.at[:, pl.ds(4 * j, 4)], v_sem.at[j])
        )
        loads[j].start()
    first = pl.multiple_of(ch * SUBCH, SUBCH)
    cd_load = pltpu.make_async_copy(cd_ref.at[:, pl.ds(first, SUBCH)], cdbuf, cd_sem)
    cd_load.start()

    barrier = pltpu.get_barrier_semaphore()
    for other in (up, down, far):
        pl.semaphore_signal(barrier, inc=1, device_id={"feed": other}, device_id_type=MESH)
    pl.semaphore_signal(barrier, inc=1, device_id={"section": 1 - sec}, device_id_type=MESH)

    @pl.loop(1, CHANS)
    def _(i):
        pl.semaphore_signal(
            barrier, inc=1, device_id={"chan": lax.rem(ch + i, CHANS)}, device_id_type=MESH
        )

    low_half = lane_ids((256, 128)) < LOCAL
    for j in range(CHUNKS):
        loads[j].wait()
        for part in range(2):
            for pair in range(2):
                for tile in range(2):
                    lanes = pl.ds(128 * tile, 128)
                    a = vbuf[part, 4 * j + 2 * pair, :, lanes]
                    b = vbuf[part, 4 * j + 2 * pair + 1, :, lanes]
                    even = jnp.where(low_half, a, pltpu.roll(b, LOCAL, 1))
                    odd = jnp.where(low_half, pltpu.roll(a, LOCAL, 1), b)
                    rows = pl.ds(256 * part, 256)
                    packed[2 * tile, j, rows, pl.ds(128 * pair, 128)] = even
                    packed[2 * tile + 1, j, rows, pl.ds(128 * pair, 128)] = odd

    pl.semaphore_wait(barrier, 3 + 1 + CHANS - 1)

    def to_feed(src, dst, sems, index, other):
        copy = pltpu.make_async_remote_copy(
            src_ref=src, dst_ref=dst, send_sem=sems[0].at[index], recv_sem=sems[1].at[index],
            device_id={"feed": other}, device_id_type=MESH,
        )
        copy.start()
        return copy

    a_sems = (a_send, a_recv)
    halves_up, halves_down, direct_up, direct_down, passed_up, passed_down = [], [], [], [], [], []
    re_rows, im_rows = pl.ds(0, 256), pl.ds(256, 256)
    for j in range(CHUNKS):
        halves_up.append(to_feed(packed.at[far, j, re_rows], relay_up.at[j], a_sems, 6 * j, up))
        halves_down.append(to_feed(packed.at[far, j, im_rows], relay_down.at[j], a_sems, 6 * j + 1, down))
    for j in range(CHUNKS):
        direct_up.append(to_feed(packed.at[up, j], arrived.at[j, 0], a_sems, 6 * j + 2, up))
        direct_down.append(to_feed(packed.at[down, j], arrived.at[j, 1], a_sems, 6 * j + 3, down))

    step = 2.0 * math.pi / NF
    for q, owner in enumerate((fd, down, up, far)):
        place = jnp.concatenate(
            [pos_ref[pl.ds(2 * owner, 1), :], pos_ref[pl.ds(2 * owner + 1, 1), :]], axis=1
        )
        ids = row_ids((32, 256))
        fine = ((ids * place) & (NF - 1)).astype(F32) * step
        coarse = ((ids * 32 * place) & (NF - 1)).astype(F32) * step
        trig[0] = jnp.cos(coarse)
        trig[1] = jnp.sin(coarse)
        trig[2] = jnp.cos(fine)
        trig[3] = jnp.sin(fine)

        @pl.loop(0, CHANS // 2)
        def _(i):
            cos_c = jnp.concatenate(
                [jnp.broadcast_to(trig[0, pl.ds(2 * i + n, 1), :], (8, 256)) for n in range(2)], axis=0
            )
            sin_c = jnp.concatenate(
                [jnp.broadcast_to(trig[1, pl.ds(2 * i + n, 1), :], (8, 256)) for n in range(2)], axis=0
            )
            for f in range(FEEDS):
                cos_f = jnp.concatenate([trig[2, 8 * f : 8 * f + 8, :]] * 2, axis=0)
                sin_f = jnp.concatenate([trig[3, 8 * f : 8 * f + 8, :]] * 2, axis=0)
                cosine = (cos_c * cos_f - sin_c * sin_f).astype(BF16)
                sine = sin_c * cos_f + cos_c * sin_f
                upper = pl.ds(pl.multiple_of(256 * f + 16 * i, 16), 16)
                lower = pl.ds(pl.multiple_of(NF + 256 * f + 16 * i, 16), 16)
                table[q, upper, 0:256] = cosine
                table[q, upper, 256:512] = sine.astype(BF16)
                table[q, lower, 0:256] = (-sine).astype(BF16)
                table[q, lower, 256:512] = cosine

    def block_dot(q, rows, right):
        return jnp.dot(table[q, rows, :], right, preferred_element_type=F32)

    for j in range(CHUNKS):
        @pl.loop(0, 4)
        def _(m):
            rows = pl.ds(pl.multiple_of(512 * m, 512), 512)
            acc[j, rows, :] = block_dot(0, rows, packed[fd, j])

    for j in range(CHUNKS):
        halves_up[j].wait_recv()
        passed_up.append(to_feed(relay_up.at[j], arrived.at[j, 2, re_rows], a_sems, 6 * j + 4, up))
        halves_down[j].wait_recv()
        passed_down.append(to_feed(relay_down.at[j], arrived.at[j, 2, im_rows], a_sems, 6 * j + 5, down))

    cd_load.wait()
    one_k = (row_ids((NK, 256)) == (lane_ids((NK, 256)) & (NK - 1))).astype(BF16)
    delay_t[...] = lax.dot_general(
        cdbuf[...].astype(F32).astype(BF16), one_k, (((0,), (0,)), ((), ())), preferred_element_type=F32
    )
    mine = delay_t[pl.ds(pl.multiple_of(fd * LOCAL, LOCAL), LOCAL), :]
    lanes = lane_ids((LOCAL, 256))
    turned = (lanes & 128) // 16 + (((lanes & 127) // 16 + 8 - lax.rem(ch, 8)) & 7)
    turned = turned.astype(F32)
    for t in range(SPAN):
        hit = (turned + mine) == float(t + D1MAX)
        chooser[LOCAL * t : LOCAL * (t + 1), :] = jnp.where(hit, 1.0, 0.0).astype(BF16)

    own_k = row_ids((NK, ND)) == lane_ids((NK, ND)) * NK // ND

    @pl.loop(0, CHANS)
    def _(s):
        delay = jnp.broadcast_to(sd_ref[pl.ds(s, 1), :], (NK, ND))
        rows = pl.ds(pl.multiple_of(NK * s, NK), NK)
        for d in range(D2MAX + 1):
            weights[d, rows, :] = jnp.where(own_k & (delay == d), 1.0, 0.0).astype(BF16)

    for j in range(CHUNKS):
        direct_up[j].wait_recv()
        direct_down[j].wait_recv()

        @pl.loop(0, 4)
        def _(m):
            rows = pl.ds(pl.multiple_of(512 * m, 512), 512)
            acc[j, rows, :] += block_dot(1, rows, arrived[j, 0]) + block_dot(2, rows, arrived[j, 1])

    def beam_power(j, f):
        rows = pl.ds(pl.multiple_of(256 * f, 256), 256)
        lower = pl.ds(pl.multiple_of(NF + 256 * f, 256), 256)
        right = arrived[j, 2]
        re = acc[j, rows, :] + block_dot(3, rows, right)
        im = acc[j, lower, :] + block_dot(3, lower, right)
        power[rows, 256 * j : 256 * (j + 1)] = re * re + im * im

    for j in range(CHUNKS):
        passed_up[j].wait_recv()
        passed_down[j].wait_recv()
        if j < CHUNKS - 1:
            @pl.loop(0, FEEDS)
            def _(f):
                beam_power(j, f)

    order = (far, up, down, fd)
    base_copies = []
    for n, f in enumerate(order):
        beam_power(CHUNKS - 1, f)
        rows = pl.ds(pl.multiple_of(256 * f, 256), 256)
        total = power[rows, 0:128]
        for tile in range(1, 6):
            total = total + power[rows, 128 * tile : 128 * (tile + 1)]
        base_own[n] = total + pltpu.roll(total, LOCAL, 1)
        copy = pltpu.make_async_remote_copy(
            src_ref=base_own.at[n], dst_ref=base_other.at[n], send_sem=b_send.at[n], recv_sem=b_recv.at[n],
            device_id={"section": 1 - sec}, device_id_type=MESH,
        )
        copy.start()
        base_copies.append(copy)

    part_copies = []
    own = None
    for n, f in enumerate(order):
        base_copies[n].wait_recv()
        rows = pl.ds(pl.multiple_of(256 * f, 256), 256)
        scale = 1.0 / ((base_own[n] + base_other[n]) * (1.0 / TT) + EPSILON)
        summed = None
        for tile in range(3):
            normed = jnp.concatenate(
                [power[rows, 256 * tile + 128 * h : 256 * tile + 128 * (h + 1)] * scale - 1.0 for h in range(2)],
                axis=1,
            )
            high = normed.astype(BF16)
            low = (normed - high.astype(F32)).astype(BF16)
            chosen = chooser[256 * tile : 256 * (tile + 1), :]
            term = jnp.dot(high, chosen, preferred_element_type=F32) + jnp.dot(
                low, chosen, preferred_element_type=F32
            )
            summed = term if summed is None else summed + term
        blocks = jnp.concatenate(
            [summed[:, 0:128].reshape(CHANS, 8, 128), summed[:, 128:256].reshape(CHANS, 8, 128)], axis=1
        )
        if n < 3:
            part_send[n] = blocks.astype(BF16)
            part_copies.append(to_feed(part_send.at[n], part_recv.at[n], (p_send, p_recv), n, f))
        else:
            own = blocks
    for copy in part_copies:
        copy.wait_recv()
    for n in range(3):
        own = own + part_recv[n].astype(F32)
    block_send[...] = own.astype(BF16)

    def chan_copy(i):
        other = lax.rem(ch + i, CHANS)
        return pltpu.make_async_remote_copy(
            src_ref=block_send.at[other], dst_ref=block_recv.at[ch],
            send_sem=q_send.at[other], recv_sem=q_recv.at[ch],
            device_id={"chan": other}, device_id_type=MESH,
        )

    @pl.loop(1, CHANS)
    def _(i):
        chan_copy(i).start()

    block_recv[ch] = block_send[ch]
    lhs[0:32, :] = jnp.zeros((32, 512), F32)
    lhs[144:176, :] = jnp.zeros((32, 512), F32)

    @pl.loop(1, CHANS)
    def _(i):
        other = lax.rem(ch + i, CHANS)
        pltpu.make_async_remote_copy(
            src_ref=block_send.at[other], dst_ref=block_recv.at[other],
            send_sem=q_send.at[other], recv_sem=q_recv.at[other],
            device_id={"chan": other}, device_id_type=MESH,
        ).wait_recv()

    spot = lane_ids((8, 128)) // 16
    for g in range(4):
        wide = [block_recv[8 * g + s].astype(F32) for s in range(8)]
        for u in range(SPAN + D1MAX):
            h = u // 8
            mixed = wide[0][8 * h : 8 * h + 8]
            for s in range(1, 8):
                mixed = jnp.where(spot == (u + s) % 8, wide[s][8 * h : 8 * h + 8], mixed)
            shift = (128 - 16 * (u % 8)) % 128
            if shift:
                mixed = pltpu.roll(mixed, shift, 1)
            lhs[32 + 8 * u : 40 + 8 * u, 128 * g : 128 * (g + 1)] = mixed

    found = None
    for d in range(D2MAX + 1):
        term = jnp.dot(lhs[8 * d : 8 * d + 8 * SPAN_V, :].astype(BF16), weights[d], preferred_element_type=F32)
        found = term if found is None else found + term
    found = found * (1.0 / math.sqrt(C))
    swap_send[...] = found[0 : 8 * SPAN]
    swap = pltpu.make_async_remote_copy(
        src_ref=swap_send, dst_ref=swap_recv, send_sem=s_send, recv_sem=s_recv,
        device_id={"section": 1 - sec}, device_id_type=MESH,
    )
    swap.start()
    out_ref[0 : 8 * SPAN, :] = found[8 * BOXMAX : 8 * SPAN_V]
    out_ref[8 * SPAN : 8 * SPAN_V, :] = jnp.zeros((8 * BOXMAX, ND), F32)
    swap.wait_recv()
    taken = jnp.where(jnp.full((8 * SPAN, ND), sec, jnp.int32) == 0, swap_recv[...], 0.0)
    out_ref[8 * BOXMAX : 8 * SPAN_V, :] += taken

    for group in (halves_up, halves_down, direct_up, direct_down, passed_up, passed_down):
        for copy in group:
            copy.wait_send()
    for copy in base_copies + part_copies:
        copy.wait_send()

    @pl.loop(1, CHANS)
    def _(i):
        chan_copy(i).wait_send()

    swap.wait_send()


def search(voltages, positions, chan_delays, sub_delays):
    vmem, anywhere = pl.BlockSpec(memory_space=pltpu.VMEM), pl.BlockSpec(memory_space=pl.ANY)
    dma = pltpu.SemaphoreType.DMA
    return pl.pallas_call(
        kernel,
        out_shape=jax.ShapeDtypeStruct((8 * SPAN_V, ND), F32),
        in_specs=[anywhere, vmem, anywhere, vmem],
        out_specs=vmem,
        scratch_shapes=[
            pltpu.VMEM((2, SPAN, 256, 256), BF16),
            pltpu.VMEM((4, CHUNKS, 512, 256), BF16),
            pltpu.VMEM((CHUNKS, 3, 512, 256), BF16),
            pltpu.VMEM((CHUNKS, 256, 256), BF16),
            pltpu.VMEM((CHUNKS, 256, 256), BF16),
            pltpu.VMEM((4, 2 * NF, 512), BF16),
            pltpu.VMEM((CHUNKS, 2 * NF, 256), F32),
            pltpu.VMEM((NF, SPAN * LOCAL), F32),
            pltpu.VMEM((4, 256, 128), F32),
            pltpu.VMEM((4, 256, 128), F32),
            pltpu.VMEM((NK, SUBCH), jnp.int32),
            pltpu.VMEM((SUBCH, 256), F32),
            pltpu.VMEM((SPAN * LOCAL, 256), BF16),
            pltpu.VMEM((D2MAX + 1, 512, ND), BF16),
            pltpu.VMEM((3, CHANS, 16, 128), BF16),
            pltpu.VMEM((3, CHANS, 16, 128), BF16),
            pltpu.VMEM((CHANS, 16, 128), BF16),
            pltpu.VMEM((CHANS, 16, 128), BF16),
            pltpu.VMEM((176, 512), F32),
            pltpu.VMEM((8 * SPAN, ND), F32),
            pltpu.VMEM((8 * SPAN, ND), F32),
            pltpu.VMEM((4, 32, 256), F32),
            dma((CHUNKS,)),
            dma,
            dma((6 * CHUNKS,)),
            dma((6 * CHUNKS,)),
            dma((4,)),
            dma((4,)),
            dma((3,)),
            dma((3,)),
            dma((CHANS,)),
            dma((CHANS,)),
            dma,
            dma,
        ],
        compiler_params=pltpu.CompilerParams(
            collective_id=0, has_side_effects=True, vmem_limit_bytes=60 * 1024 * 1024
        ),
        name="search",
    )(
        jnp.transpose(voltages, (0, 2, 1, 3)),
        positions.reshape(8, 128),
        chan_delays,
        jnp.transpose(sub_delays),
    )


def boxcar_kernel(box_ref, ext_ref, out_ref):
    for filter_index in range(NW):
        width_now = box_ref[0, filter_index]
        stride_now = box_ref[1, filter_index]
        gain = lax.rsqrt(jnp.full((8, ND), width_now, jnp.int32).astype(F32))
        summed = ext_ref[0:SPAN]
        for offset in range(1, NW + 1):
            start = jnp.minimum(offset * stride_now, BOXMAX)
            kept = jnp.where(offset < width_now, 1.0, 0.0)
            summed = summed + ext_ref[pl.ds(start, SPAN)] * kept
        out_ref[:, filter_index] = summed * gain[None]


def boxcar_filter(extended, boxcars):
    vmem = pl.BlockSpec(memory_space=pltpu.VMEM)
    filtered = pl.pallas_call(
        boxcar_kernel,
        out_shape=jax.ShapeDtypeStruct((SPAN, NW, 8, ND), F32),
        in_specs=[pl.BlockSpec(memory_space=pltpu.SMEM), vmem],
        out_specs=vmem,
        name="boxcar",
    )(jnp.transpose(boxcars), extended)
    return jnp.transpose(filtered, (2, 0, 1, 3))


def per_device(voltages, positions, chan_delays, sub_delays, boxcars):
    extended = search(voltages, positions, chan_delays, sub_delays)
    return boxcar_filter(extended.reshape(SPAN_V, 8, ND), boxcars)


def solution(mesh):
    return jax.shard_map(
        per_device,
        mesh=mesh,
        in_specs=(P(None, "feed", "section", "chan"), P(), P(), P(), P()),
        out_specs=P(("chan", "feed"), "section", None, None),
        check_vma=False,
    )
```

```python
import math

import jax
import jax.numpy as jnp
from jax import lax
from jax.experimental import pallas as pl
from jax.experimental.pallas import tpu as pltpu
from jax.sharding import PartitionSpec as P

NF = 1024
C = 8192
NK = 16
ND = 256
NW = 3
D1MAX = 2
D2MAX = 4
BOXMAX = 6
TT = 24
SUBCH = 256
EPSILON = 1e-05

SPAN = 12
LOCAL = 64
CHANS = 32
FEEDS = 4
CHUNKS = 3
SPAN_V = SPAN + BOXMAX
F32 = jnp.float32
BF16 = jnp.bfloat16
MESH = pl.DeviceIdType.MESH


def lane_ids(shape):
    return lax.broadcasted_iota(jnp.int32, shape, len(shape) - 1)


def row_ids(shape):
    return lax.broadcasted_iota(jnp.int32, shape, len(shape) - 2)


def kernel(
    v_ref, pos_ref, cd_ref, sd_ref, out_ref,
    vbuf, packed, arrived, relay_up, relay_down, table, acc, power,
    rim, base_own, base_other, cdbuf, delay_t, chooser, weights,
    part_send, part_recv, block_send, block_recv, lhs, swap_send, swap_recv, trig,
    v_sem, cd_sem, a_send, a_recv, r_send, r_recv, b_send, b_recv, p_send, p_recv, q_send, q_recv, s_send, s_recv,
):
    sec = lax.axis_index("section")
    ch = lax.axis_index("chan")
    fd = lax.axis_index("feed")
    zed, ex = lax.div(ch, 4), lax.rem(ch, 4)
    up, down, far = lax.rem(fd + 1, 4), lax.rem(fd + 3, 4), lax.rem(fd + 2, 4)

    loads = []
    for j in range(CHUNKS):
        loads.append(
            pltpu.make_async_copy(v_ref.at[:, pl.ds(4 * j, 4)], vbuf.at[:, pl.ds(4 * j, 4)], v_sem.at[j])
        )
        loads[j].start()
    first = pl.multiple_of(ch * SUBCH, SUBCH)
    cd_load = pltpu.make_async_copy(cd_ref.at[:, pl.ds(first, SUBCH)], cdbuf, cd_sem)
    cd_load.start()

    barrier = pltpu.get_barrier_semaphore()
    for other in (up, down, far):
        pl.semaphore_signal(barrier, inc=1, device_id={"feed": other}, device_id_type=MESH)
    pl.semaphore_signal(barrier, inc=1, device_id={"section": 1 - sec}, device_id_type=MESH)

    @pl.loop(1, CHANS)
    def _(i):
        pl.semaphore_signal(
            barrier, inc=1, device_id={"chan": lax.rem(ch + i, CHANS)}, device_id_type=MESH
        )

    low_half = lane_ids((256, 128)) < LOCAL
    for j in range(CHUNKS):
        loads[j].wait()
        for part in range(2):
            for pair in range(2):
                for tile in range(2):
                    lanes = pl.ds(128 * tile, 128)
                    a = vbuf[part, 4 * j + 2 * pair, :, lanes]
                    b = vbuf[part, 4 * j + 2 * pair + 1, :, lanes]
                    even = jnp.where(low_half, a, pltpu.roll(b, LOCAL, 1))
                    odd = jnp.where(low_half, pltpu.roll(a, LOCAL, 1), b)
                    rows = pl.ds(256 * part, 256)
                    packed[2 * tile, j, rows, pl.ds(128 * pair, 128)] = even
                    packed[2 * tile + 1, j, rows, pl.ds(128 * pair, 128)] = odd

    pl.semaphore_wait(barrier, 3 + 1 + CHANS - 1)

    def to_feed(src, dst, sems, index, other):
        copy = pltpu.make_async_remote_copy(
            src_ref=src, dst_ref=dst, send_sem=sems[0].at[index], recv_sem=sems[1].at[index],
            device_id={"feed": other}, device_id_type=MESH,
        )
        copy.start()
        return copy

    a_sems = (a_send, a_recv)
    halves_up, halves_down, direct_up, direct_down, passed_up, passed_down = [], [], [], [], [], []
    re_rows, im_rows = pl.ds(0, 256), pl.ds(256, 256)
    for j in range(CHUNKS):
        halves_up.append(to_feed(packed.at[far, j, re_rows], relay_up.at[j], a_sems, 6 * j, up))
        halves_down.append(to_feed(packed.at[far, j, im_rows], relay_down.at[j], a_sems, 6 * j + 1, down))
    for j in range(CHUNKS):
        direct_up.append(to_feed(packed.at[up, j], arrived.at[j, 0], a_sems, 6 * j + 2, up))
        direct_down.append(to_feed(packed.at[down, j], arrived.at[j, 1], a_sems, 6 * j + 3, down))

    step = 2.0 * math.pi / NF
    for q, owner in enumerate((fd, down, up, far)):
        place = jnp.concatenate(
            [pos_ref[pl.ds(2 * owner, 1), :], pos_ref[pl.ds(2 * owner + 1, 1), :]], axis=1
        )
        ids = row_ids((32, 256))
        fine = ((ids * place) & (NF - 1)).astype(F32) * step
        coarse = ((ids * 32 * place) & (NF - 1)).astype(F32) * step
        trig[0] = jnp.cos(coarse)
        trig[1] = jnp.sin(coarse)
        trig[2] = jnp.cos(fine)
        trig[3] = jnp.sin(fine)

        @pl.loop(0, CHANS // 2)
        def _(i):
            hop = lax.div(i, 2)
            pair = lax.rem(i, 2)
            chan = lax.rem(zed + hop + 2, 8) * 4 + 2 * pair
            base = lax.div(hop, 4) * 512 + lax.rem(hop, 4) * 32 + pair * 16
            cos_c = jnp.concatenate(
                [jnp.broadcast_to(trig[0, pl.ds(chan + n, 1), :], (8, 256)) for n in range(2)], axis=0
            )
            sin_c = jnp.concatenate(
                [jnp.broadcast_to(trig[1, pl.ds(chan + n, 1), :], (8, 256)) for n in range(2)], axis=0
            )
            for f in range(FEEDS):
                cos_f = jnp.concatenate([trig[2, 8 * f : 8 * f + 8, :]] * 2, axis=0)
                sin_f = jnp.concatenate([trig[3, 8 * f : 8 * f + 8, :]] * 2, axis=0)
                cosine = (cos_c * cos_f - sin_c * sin_f).astype(BF16)
                sine = sin_c * cos_f + cos_c * sin_f
                upper = pl.ds(pl.multiple_of(128 * f + base, 16), 16)
                lower = pl.ds(pl.multiple_of(NF + 128 * f + base, 16), 16)
                table[q, upper, 0:256] = cosine
                table[q, upper, 256:512] = sine.astype(BF16)
                table[q, lower, 0:256] = (-sine).astype(BF16)
                table[q, lower, 256:512] = cosine

    def block_dot(q, rows, right):
        return jnp.dot(table[q, rows, :], right, preferred_element_type=F32)

    for j in range(CHUNKS):
        @pl.loop(0, 4)
        def _(m):
            rows = pl.ds(pl.multiple_of(512 * m, 512), 512)
            acc[j, rows, :] = block_dot(0, rows, packed[fd, j])

    for j in range(CHUNKS):
        halves_up[j].wait_recv()
        passed_up.append(to_feed(relay_up.at[j], arrived.at[j, 2, re_rows], a_sems, 6 * j + 4, up))
        halves_down[j].wait_recv()
        passed_down.append(to_feed(relay_down.at[j], arrived.at[j, 2, im_rows], a_sems, 6 * j + 5, down))

    cd_load.wait()
    one_k = (row_ids((NK, 256)) == (lane_ids((NK, 256)) & (NK - 1))).astype(BF16)
    delay_t[...] = lax.dot_general(
        cdbuf[...].astype(F32).astype(BF16), one_k, (((0,), (0,)), ((), ())), preferred_element_type=F32
    )
    mine = delay_t[pl.ds(pl.multiple_of(fd * LOCAL, LOCAL), LOCAL), :]
    lanes = lane_ids((LOCAL, 256))
    spot = (lanes & 127) // 16
    early = (spot + 8 - lax.rem(ch, 8)) & 7
    u_of = jnp.where(lanes < 128, early, 8 + (spot & 3)).astype(F32)
    for t in range(SPAN + D1MAX):
        hit = (u_of + mine) == float(t)
        if t >= SPAN:
            hit = hit & (jnp.full((LOCAL, 256), sec, jnp.int32) == 0)
        chooser[LOCAL * t : LOCAL * (t + 1), :] = jnp.where(hit, 1.0, 0.0).astype(BF16)

    own_k = row_ids((NK, ND)) == lane_ids((NK, ND)) * NK // ND

    @pl.loop(0, CHANS)
    def _(s):
        delay = jnp.broadcast_to(sd_ref[pl.ds(s, 1), :], (NK, ND))
        rows = pl.ds(pl.multiple_of(NK * s, NK), NK)
        for d in range(D2MAX + 1):
            weights[d, rows, :] = jnp.where(own_k & (delay == d), 1.0, 0.0).astype(BF16)

    for j in range(CHUNKS):
        direct_up[j].wait_recv()
        direct_down[j].wait_recv()

        @pl.loop(0, 4)
        def _(m):
            rows = pl.ds(pl.multiple_of(512 * m, 512), 512)
            acc[j, rows, :] += block_dot(1, rows, arrived[j, 0]) + block_dot(2, rows, arrived[j, 1])

    def beam_power(j, m):
        rows = pl.ds(pl.multiple_of(512 * m, 512), 512)
        lower = pl.ds(pl.multiple_of(NF + 512 * m, 512), 512)
        right = arrived[j, 2]
        re = acc[j, rows, :] + block_dot(3, rows, right)
        im = acc[j, lower, :] + block_dot(3, lower, right)
        power[rows, 256 * j : 256 * (j + 1)] = re * re + im * im

    def to_core(src, dst, send_sem, recv_sem):
        copy = pltpu.make_async_remote_copy(
            src_ref=src, dst_ref=dst, send_sem=send_sem, recv_sem=recv_sem,
            device_id={"section": 1 - sec}, device_id_type=MESH,
        )
        copy.start()
        return copy

    rim_copy = None
    for j in range(CHUNKS - 1):
        passed_up[j].wait_recv()
        passed_down[j].wait_recv()

        @pl.loop(0, 2)
        def _(m):
            beam_power(j, m)

        if j == 0:
            rim_copy = to_core(power.at[:, pl.ds(0, 128)], rim, r_send, r_recv)

    passed_up[CHUNKS - 1].wait_recv()
    passed_down[CHUNKS - 1].wait_recv()
    base_copies = []
    for h in range(2):
        beam_power(CHUNKS - 1, h)
        rows = pl.ds(512 * h, 512)
        total = power[rows, 0:128]
        for tile in range(1, 6):
            total = total + power[rows, 128 * tile : 128 * (tile + 1)]
        base_own[h] = total + pltpu.roll(total, LOCAL, 1)
        base_copies.append(to_core(base_own.at[h], base_other.at[h], b_send.at[h], b_recv.at[h]))

    rim_copy.wait_recv()
    low_lanes = lane_ids((2, 4, 2, 8, 128)) < LOCAL
    part_copies, owns = [], []
    for h in range(2):
        base_copies[h].wait_recv()
        copies = []
        for pair in ((far, up), (down, fd)):
            tiles = [[] for _ in range(7)]
            for f in pair:
                within = pl.ds(pl.multiple_of(128 * f, 128), 128)
                rows = pl.ds(pl.multiple_of(512 * h + 128 * f, 128), 128)
                scale = 1.0 / ((base_own[h, within] + base_other[h, within]) * (1.0 / TT) + EPSILON)
                for tile in range(7):
                    part = power[rows, 128 * tile : 128 * (tile + 1)] if tile < 6 else rim[rows, :]
                    tiles[tile].append(part * scale - 1.0)
            tiles = [jnp.concatenate(parts, axis=0) for parts in tiles]
            summed = None
            for tile in range(4):
                normed = jnp.concatenate(tiles[2 * tile : 2 * tile + 2], axis=1)
                high = normed.astype(BF16)
                low = (normed - high.astype(F32)).astype(BF16)
                chosen = chooser[256 * tile : 256 * tile + normed.shape[1], :]
                term = jnp.dot(jnp.concatenate([high, low], axis=0), chosen, preferred_element_type=F32)
                summed = term if summed is None else summed + term
            summed = summed[0:256] + summed[256:512]
            early = summed[:, 0:128].reshape(2, 4, 32, 128)
            late = summed[:, 128:256].reshape(2, 4, 2, 2, 8, 128)
            late = jnp.where(low_lanes, late[:, :, :, 0], late[:, :, :, 1]).reshape(2, 4, 16, 128)
            blocks = jnp.concatenate([early, late], axis=2)
            for a in range(2):
                n = len(copies)
                if n < 3:
                    part_send[h, n] = blocks[a].astype(BF16)
                    copies.append(
                        to_feed(part_send.at[h, n], part_recv.at[h, n], (p_send, p_recv), 3 * h + n, pair[a])
                    )
                else:
                    owns.append(blocks[a])
        part_copies.append(copies)

    chan_copies = []
    for h in range(2):
        total = owns[h]
        for n in range(3):
            part_copies[h][n].wait_recv()
            total = total + part_recv[h, n].astype(F32)
        for x in range(4):
            late = total[:, 32 + 8 * (x // 2) : 40 + 8 * (x // 2)].reshape(32, 128)
            if x % 2:
                late = pltpu.roll(late, LOCAL, 1)
            block = jnp.concatenate([total[:, 8 * x : 8 * x + 8], late.reshape(4, 8, 128)], axis=1)
            block_send[4 * h : 4 * h + 4, x] = block.astype(BF16)
        for a in range(4):
            hop = (4 * h + a + 2) % 8
            for i in ((2, 1, 3) if hop == 0 else (2, 1, 3, 0)):
                x = lax.rem(ex + i, 4)
                other = lax.rem(zed + hop, 8) * 4 + x
                copy = pltpu.make_async_remote_copy(
                    src_ref=block_send.at[4 * h + a, x], dst_ref=block_recv.at[ch],
                    send_sem=q_send.at[4 * (4 * h + a) + i], recv_sem=q_recv.at[ch],
                    device_id={"chan": other}, device_id_type=MESH,
                )
                copy.start()
                chan_copies.append(copy)

    block_recv[ch] = block_send[6, ex]
    lhs[0:32, :] = jnp.zeros((32, 512), F32)
    lhs[128:160, :] = jnp.zeros((32, 512), F32)

    @pl.loop(1, CHANS)
    def _(i):
        other = lax.rem(ch + i, CHANS)
        pltpu.make_async_remote_copy(
            src_ref=block_send.at[0, 0], dst_ref=block_recv.at[other],
            send_sem=q_send.at[0], recv_sem=q_recv.at[other],
            device_id={"chan": other}, device_id_type=MESH,
        ).wait_recv()

    spot = lane_ids((8, 128)) // 16
    for g in range(4):
        wide = [block_recv[8 * g + s].astype(F32) for s in range(8)]
        for u in range(SPAN):
            if u < 8:
                mixed = wide[0][0:8]
                for s in range(1, 8):
                    mixed = jnp.where(spot == (u + s) % 8, wide[s][0:8], mixed)
                if u:
                    mixed = pltpu.roll(mixed, 128 - 16 * u, 1)
            else:
                mixed = None
                for s in range(8):
                    shift = (16 * (s - (u - 8))) % 128
                    moved = pltpu.roll(wide[s][8:16], shift, 1) if shift else wide[s][8:16]
                    mixed = moved if mixed is None else jnp.where(spot == s, moved, mixed)
            lhs[32 + 8 * u : 40 + 8 * u, 128 * g : 128 * (g + 1)] = mixed

    found = None
    for d in range(D2MAX + 1):
        term = jnp.dot(lhs[8 * d : 8 * d + 128, :].astype(BF16), weights[d], preferred_element_type=F32)
        found = term if found is None else found + term
    found = found * (1.0 / math.sqrt(C))
    swap_send[...] = found[0:80]
    swap = to_core(swap_send, swap_recv, s_send, s_recv)
    out_ref[0 : 8 * SPAN, :] = found[32:128]
    out_ref[8 * SPAN : 8 * SPAN_V, :] = jnp.zeros((8 * BOXMAX, ND), F32)
    swap.wait_recv()
    taken = jnp.where(jnp.full((80, ND), sec, jnp.int32) == 0, swap_recv[...], 0.0)
    out_ref[64 : 8 * SPAN_V, :] += taken

    for group in (halves_up, halves_down, direct_up, direct_down, passed_up, passed_down):
        for copy in group:
            copy.wait_send()
    for copy in base_copies + part_copies[0] + part_copies[1]:
        copy.wait_send()
    for copy in chan_copies:
        copy.wait_send()
    rim_copy.wait_send()
    swap.wait_send()


def search(voltages, positions, chan_delays, sub_delays):
    vmem, anywhere = pl.BlockSpec(memory_space=pltpu.VMEM), pl.BlockSpec(memory_space=pl.ANY)
    dma = pltpu.SemaphoreType.DMA
    return pl.pallas_call(
        kernel,
        out_shape=jax.ShapeDtypeStruct((8 * SPAN_V, ND), F32),
        in_specs=[anywhere, vmem, anywhere, vmem],
        out_specs=vmem,
        scratch_shapes=[
            pltpu.VMEM((2, SPAN, 256, 256), BF16),
            pltpu.VMEM((4, CHUNKS, 512, 256), BF16),
            pltpu.VMEM((CHUNKS, 3, 512, 256), BF16),
            pltpu.VMEM((CHUNKS, 256, 256), BF16),
            pltpu.VMEM((CHUNKS, 256, 256), BF16),
            pltpu.VMEM((4, 2 * NF, 512), BF16),
            pltpu.VMEM((CHUNKS, 2 * NF, 256), F32),
            pltpu.VMEM((NF, SPAN * LOCAL), F32),
            pltpu.VMEM((NF, 128), F32),
            pltpu.VMEM((2, 512, 128), F32),
            pltpu.VMEM((2, 512, 128), F32),
            pltpu.VMEM((NK, SUBCH), jnp.int32),
            pltpu.VMEM((SUBCH, 256), F32),
            pltpu.VMEM(((SPAN + D1MAX) * LOCAL, 256), BF16),
            pltpu.VMEM((D2MAX + 1, 512, ND), BF16),
            pltpu.VMEM((2, 3, 4, 48, 128), BF16),
            pltpu.VMEM((2, 3, 4, 48, 128), BF16),
            pltpu.VMEM((8, 4, 16, 128), BF16),
            pltpu.VMEM((CHANS, 16, 128), BF16),
            pltpu.VMEM((160, 512), F32),
            pltpu.VMEM((80, ND), F32),
            pltpu.VMEM((80, ND), F32),
            pltpu.VMEM((4, 32, 256), F32),
            dma((CHUNKS,)),
            dma,
            dma((6 * CHUNKS,)),
            dma((6 * CHUNKS,)),
            dma,
            dma,
            dma((2,)),
            dma((2,)),
            dma((6,)),
            dma((6,)),
            dma((CHANS,)),
            dma((CHANS,)),
            dma,
            dma,
        ],
        compiler_params=pltpu.CompilerParams(
            collective_id=0, has_side_effects=True, vmem_limit_bytes=60 * 1024 * 1024
        ),
        name="search",
    )(
        jnp.transpose(voltages, (0, 2, 1, 3)),
        positions.reshape(8, 128),
        chan_delays,
        jnp.transpose(sub_delays),
    )


def boxcar_kernel(box_ref, ext_ref, out_ref):
    for filter_index in range(NW):
        width_now = box_ref[0, filter_index]
        stride_now = box_ref[1, filter_index]
        gain = lax.rsqrt(jnp.full((8, ND), width_now, jnp.int32).astype(F32))
        summed = ext_ref[0:SPAN]
        for offset in range(1, NW + 1):
            start = jnp.minimum(offset * stride_now, BOXMAX)
            kept = jnp.where(offset < width_now, 1.0, 0.0)
            summed = summed + ext_ref[pl.ds(start, SPAN)] * kept
        out_ref[:, filter_index] = summed * gain[None]


def boxcar_filter(extended, boxcars):
    vmem = pl.BlockSpec(memory_space=pltpu.VMEM)
    filtered = pl.pallas_call(
        boxcar_kernel,
        out_shape=jax.ShapeDtypeStruct((SPAN, NW, 8, ND), F32),
        in_specs=[pl.BlockSpec(memory_space=pltpu.SMEM), vmem],
        out_specs=vmem,
        name="boxcar",
    )(jnp.transpose(boxcars), extended)
    return jnp.transpose(filtered, (2, 0, 1, 3))


def per_device(voltages, positions, chan_delays, sub_delays, boxcars):
    extended = search(voltages, positions, chan_delays, sub_delays)
    return boxcar_filter(extended.reshape(SPAN_V, 8, ND), boxcars)


def solution(mesh):
    return jax.shard_map(
        per_device,
        mesh=mesh,
        in_specs=(P(None, "feed", "section", "chan"), P(), P(), P(), P()),
        out_specs=P(("chan", "feed"), "section", None, None),
        check_vma=False,
    )
```

```python
import math

import jax
import jax.numpy as jnp
from jax import lax
from jax.experimental import pallas as pl
from jax.experimental.pallas import tpu as pltpu
from jax.sharding import PartitionSpec as P

NF = 1024
C = 8192
NK = 16
ND = 256
NW = 3
D1MAX = 2
D2MAX = 4
BOXMAX = 6
TT = 24
SUBCH = 256
EPSILON = 1e-05

SPAN = 12
LOCAL = 64
CHANS = 32
FEEDS = 4
CHUNKS = 3
SPAN_V = SPAN + BOXMAX
F32 = jnp.float32
BF16 = jnp.bfloat16
MESH = pl.DeviceIdType.MESH


def lane_ids(shape):
    return lax.broadcasted_iota(jnp.int32, shape, len(shape) - 1)


def row_ids(shape):
    return lax.broadcasted_iota(jnp.int32, shape, len(shape) - 2)


def kernel(
    v_ref, pos_any, cd_ref, sd_any, out_ref,
    pos_ref, sd_ref, vbuf, packed, arrived, relay_up, relay_down, table, acc, power,
    rim, base_own, base_other, cdbuf, delay_t, chooser, weights,
    part_own, part_send, part_recv, block_send, block_recv, lhs, swap_send, swap_recv, trig,
    v_sem, cd_sem, pos_sem, sd_sem, a_send, a_recv, r_send, r_recv, b_send, b_recv, p_send, p_recv, q_send, q_recv, s_send, s_recv,
):
    sec = lax.axis_index("section")
    ch = lax.axis_index("chan")
    fd = lax.axis_index("feed")
    zed, ex = lax.div(ch, 4), lax.rem(ch, 4)
    up, down, far = lax.rem(fd + 1, 4), lax.rem(fd + 3, 4), lax.rem(fd + 2, 4)

    barrier = pltpu.get_barrier_semaphore()
    for other in (up, down, far):
        pl.semaphore_signal(barrier, inc=1, device_id={"feed": other}, device_id_type=MESH)
    pl.semaphore_signal(barrier, inc=1, device_id={"section": 1 - sec}, device_id_type=MESH)

    @pl.loop(1, CHANS)
    def _(i):
        pl.semaphore_signal(
            barrier, inc=1, device_id={"chan": lax.rem(ch + i, CHANS)}, device_id_type=MESH
        )

    loads = []
    for j in range(CHUNKS):
        loads.append(
            pltpu.make_async_copy(v_ref.at[:, pl.ds(4 * j, 4)], vbuf.at[:, pl.ds(4 * j, 4)], v_sem.at[j])
        )
        loads[j].start()
    first = pl.multiple_of(ch * SUBCH, SUBCH)
    cd_load = pltpu.make_async_copy(cd_ref.at[:, pl.ds(first, SUBCH)], cdbuf, cd_sem)
    cd_load.start()
    pos_load = pltpu.make_async_copy(pos_any, pos_ref, pos_sem)
    pos_load.start()
    sd_load = pltpu.make_async_copy(sd_any, sd_ref, sd_sem)
    sd_load.start()

    low_half = lane_ids((256, 128)) < LOCAL
    for j in range(CHUNKS):
        loads[j].wait()
        for part in range(2):
            for pair in range(2):
                for tile in range(2):
                    lanes = pl.ds(128 * tile, 128)
                    a = vbuf[part, 4 * j + 2 * pair, :, lanes]
                    b = vbuf[part, 4 * j + 2 * pair + 1, :, lanes]
                    even = jnp.where(low_half, a, pltpu.roll(b, LOCAL, 1))
                    odd = jnp.where(low_half, pltpu.roll(a, LOCAL, 1), b)
                    rows = pl.ds(256 * part, 256)
                    packed[2 * tile, j, rows, pl.ds(128 * pair, 128)] = even
                    packed[2 * tile + 1, j, rows, pl.ds(128 * pair, 128)] = odd

    pl.semaphore_wait(barrier, 3 + 1 + CHANS - 1)

    def to_feed(src, dst, sems, index, other):
        copy = pltpu.make_async_remote_copy(
            src_ref=src, dst_ref=dst, send_sem=sems[0].at[index], recv_sem=sems[1].at[index],
            device_id={"feed": other}, device_id_type=MESH,
        )
        copy.start()
        return copy

    a_sems = (a_send, a_recv)
    halves_up, halves_down, direct_up, direct_down, passed_up, passed_down = [], [], [], [], [], []
    re_rows, im_rows = pl.ds(0, 256), pl.ds(256, 256)
    for j in range(CHUNKS):
        halves_up.append(to_feed(packed.at[far, j, re_rows], relay_up.at[j], a_sems, 6 * j, up))
        halves_down.append(to_feed(packed.at[far, j, im_rows], relay_down.at[j], a_sems, 6 * j + 1, down))
    for j in range(CHUNKS):
        direct_up.append(to_feed(packed.at[up, j], arrived.at[j, 0], a_sems, 6 * j + 2, up))
        direct_down.append(to_feed(packed.at[down, j], arrived.at[j, 1], a_sems, 6 * j + 3, down))

    step = 2.0 * math.pi / NF
    pos_load.wait()
    for q, owner in enumerate((fd, down, up, far)):
        place = jnp.concatenate(
            [pos_ref[pl.ds(2 * owner, 1), :], pos_ref[pl.ds(2 * owner + 1, 1), :]], axis=1
        )
        ids = row_ids((32, 256))
        fine = ((ids * place) & (NF - 1)).astype(F32) * step
        coarse = ((ids * 32 * place) & (NF - 1)).astype(F32) * step
        trig[0] = jnp.cos(coarse)
        trig[1] = jnp.sin(coarse)
        trig[2] = jnp.cos(fine)
        trig[3] = jnp.sin(fine)

        @pl.loop(0, CHANS // 2)
        def _(i):
            hop = lax.div(i, 2)
            pair = lax.rem(i, 2)
            chan = lax.rem(zed + hop + 3, 8) * 4 + 2 * pair
            base = lax.div(hop, 2) * 256 + lax.rem(hop, 2) * 32 + pair * 16
            cos_c = jnp.concatenate(
                [jnp.broadcast_to(trig[0, pl.ds(chan + n, 1), :], (8, 256)) for n in range(2)], axis=0
            )
            sin_c = jnp.concatenate(
                [jnp.broadcast_to(trig[1, pl.ds(chan + n, 1), :], (8, 256)) for n in range(2)], axis=0
            )
            for f in range(FEEDS):
                cos_f = jnp.concatenate([trig[2, 8 * f : 8 * f + 8, :]] * 2, axis=0)
                sin_f = jnp.concatenate([trig[3, 8 * f : 8 * f + 8, :]] * 2, axis=0)
                cosine = (cos_c * cos_f - sin_c * sin_f).astype(BF16)
                sine = sin_c * cos_f + cos_c * sin_f
                upper = pl.ds(pl.multiple_of(64 * f + base, 16), 16)
                lower = pl.ds(pl.multiple_of(NF + 64 * f + base, 16), 16)
                table[q, upper, 0:256] = cosine
                table[q, upper, 256:512] = sine.astype(BF16)
                table[q, lower, 0:256] = (-sine).astype(BF16)
                table[q, lower, 256:512] = cosine

    def block_dot(q, rows, right):
        return jnp.dot(table[q, rows, :], right, preferred_element_type=F32)

    for j in range(CHUNKS):
        @pl.loop(0, 4)
        def _(m):
            rows = pl.ds(pl.multiple_of(512 * m, 512), 512)
            acc[j, rows, :] = block_dot(0, rows, packed[fd, j])

    for j in range(CHUNKS):
        halves_up[j].wait_recv()
        passed_up.append(to_feed(relay_up.at[j], arrived.at[j, 2, re_rows], a_sems, 6 * j + 4, up))
        halves_down[j].wait_recv()
        passed_down.append(to_feed(relay_down.at[j], arrived.at[j, 2, im_rows], a_sems, 6 * j + 5, down))

    cd_load.wait()
    one_k = (row_ids((NK, 256)) == (lane_ids((NK, 256)) & (NK - 1))).astype(BF16)
    delay_t[...] = lax.dot_general(
        cdbuf[...].astype(F32).astype(BF16), one_k, (((0,), (0,)), ((), ())), preferred_element_type=F32
    )
    mine = delay_t[pl.ds(pl.multiple_of(fd * LOCAL, LOCAL), LOCAL), :]
    lanes = lane_ids((LOCAL, 256))
    spot = (lanes & 127) // 16
    early = (spot + 8 - lax.rem(ch, 8)) & 7
    u_of = jnp.where(lanes < 128, early, 8 + (spot & 3)).astype(F32)
    for t in range(SPAN + D1MAX):
        hit = (u_of + mine) == float(t)
        if t >= SPAN:
            hit = hit & (jnp.full((LOCAL, 256), sec, jnp.int32) == 0)
        chooser[LOCAL * t : LOCAL * (t + 1), :] = jnp.where(hit, 1.0, 0.0).astype(BF16)

    sd_load.wait()
    own_k = row_ids((NK, ND)) == lane_ids((NK, ND)) * NK // ND

    @pl.loop(0, CHANS)
    def _(s):
        delay = jnp.broadcast_to(sd_ref[pl.ds(s, 1), :], (NK, ND))
        rows = pl.ds(pl.multiple_of(NK * s, NK), NK)
        for d in range(D2MAX + 1):
            weights[d, rows, :] = jnp.where(own_k & (delay == d), 1.0, 0.0).astype(BF16)

    for j in range(CHUNKS):
        direct_up[j].wait_recv()
        direct_down[j].wait_recv()

        @pl.loop(0, 4)
        def _(m):
            rows = pl.ds(pl.multiple_of(512 * m, 512), 512)
            acc[j, rows, :] += block_dot(1, rows, arrived[j, 0]) + block_dot(2, rows, arrived[j, 1])

    def beam_power(j, m):
        rows = pl.ds(pl.multiple_of(512 * m, 512), 512)
        lower = pl.ds(pl.multiple_of(NF + 512 * m, 512), 512)
        right = arrived[j, 2]
        re = acc[j, rows, :] + block_dot(3, rows, right)
        im = acc[j, lower, :] + block_dot(3, lower, right)
        power[rows, 256 * j : 256 * (j + 1)] = re * re + im * im

    def to_core(src, dst, send_sem, recv_sem):
        copy = pltpu.make_async_remote_copy(
            src_ref=src, dst_ref=dst, send_sem=send_sem, recv_sem=recv_sem,
            device_id={"section": 1 - sec}, device_id_type=MESH,
        )
        copy.start()
        return copy

    rim_copy = None
    for j in range(CHUNKS - 1):
        passed_up[j].wait_recv()
        passed_down[j].wait_recv()

        @pl.loop(0, 2)
        def _(m):
            beam_power(j, m)

        if j == 0:
            rim_copy = to_core(power.at[:, pl.ds(0, 128)], rim, r_send, r_recv)

    passed_up[CHUNKS - 1].wait_recv()
    passed_down[CHUNKS - 1].wait_recv()
    base_copies = []
    for h in range(2):
        beam_power(CHUNKS - 1, h)
        rows = pl.ds(512 * h, 512)
        total = power[rows, 0:128]
        for tile in range(1, 6):
            total = total + power[rows, 128 * tile : 128 * (tile + 1)]
        base_own[h] = total + pltpu.roll(total, LOCAL, 1)
        base_copies.append(to_core(base_own.at[h], base_other.at[h], b_send.at[h], b_recv.at[h]))

    rim_copy.wait_recv()
    low_lanes = lane_ids((4, 2, 2, 8, 128)) < LOCAL
    part_copies = {}
    turns = (0, 1, 3, 2)
    for q in turns:
        h = q // 2
        if q in (0, 3):
            base_copies[h].wait_recv()
        within = pl.ds(256 * (q % 2), 256)
        rows = pl.ds(256 * q, 256)
        scale = 1.0 / ((base_own[h, within] + base_other[h, within]) * (1.0 / TT) + EPSILON)
        tiles = [power[rows, 128 * tile : 128 * (tile + 1)] * scale - 1.0 for tile in range(6)]
        tiles.append(rim[rows, :] * scale - 1.0)
        summed = None
        for tile in range(4):
            normed = jnp.concatenate(tiles[2 * tile : 2 * tile + 2], axis=1)
            high = normed.astype(BF16)
            low = (normed - high.astype(F32)).astype(BF16)
            chosen = chooser[256 * tile : 256 * tile + normed.shape[1], :]
            term = jnp.dot(jnp.concatenate([high, low], axis=0), chosen, preferred_element_type=F32)
            summed = term if summed is None else summed + term
        summed = summed[0:256] + summed[256:512]
        early = summed[:, 0:128].reshape(4, 2, 32, 128)
        late = summed[:, 128:256].reshape(4, 2, 2, 2, 8, 128)
        late = jnp.where(low_lanes, late[:, :, :, 0], late[:, :, :, 1]).reshape(4, 2, 16, 128)
        blocks = jnp.concatenate([early, late], axis=2)
        part_own[q] = blocks
        part_send[q] = blocks.astype(BF16)
        part_copies[q] = [
            to_feed(part_send.at[q, f], part_recv.at[q, n], (p_send, p_recv), 3 * q + n, f)
            for n, f in enumerate((far, up, down))
        ]

    lhs[0:32, :] = jnp.zeros((32, 512), F32)
    lhs[128:160, :] = jnp.zeros((32, 512), F32)

    chan_copies = []
    for q in turns:
        total = part_own[q, fd]
        for n in range(3):
            part_copies[q][n].wait_recv()
            total = total + part_recv[q, n].astype(F32)
        for x in range(4):
            late = total[:, 32 + 8 * (x // 2) : 40 + 8 * (x // 2)].reshape(16, 128)
            if x % 2:
                late = pltpu.roll(late, LOCAL, 1)
            block = jnp.concatenate([total[:, 8 * x : 8 * x + 8], late.reshape(2, 8, 128)], axis=1)
            block_send[2 * q : 2 * q + 2, x] = block.astype(BF16)
        for a in range(2):
            spot = 2 * q + a
            hop = (spot + 3) % 8
            for i in ((2, 1, 3) if hop == 0 else (2, 1, 3, 0)):
                x = lax.rem(ex + i, 4)
                other = lax.rem(zed + hop, 8) * 4 + x
                copy = pltpu.make_async_remote_copy(
                    src_ref=block_send.at[spot, x], dst_ref=block_recv.at[ch],
                    send_sem=q_send.at[4 * spot + i], recv_sem=q_recv.at[ch],
                    device_id={"chan": other}, device_id_type=MESH,
                )
                copy.start()
                chan_copies.append(copy)

    block_recv[ch] = block_send[5, ex]

    @pl.loop(1, CHANS)
    def _(i):
        other = lax.rem(ch + i, CHANS)
        pltpu.make_async_remote_copy(
            src_ref=block_send.at[0, 0], dst_ref=block_recv.at[other],
            send_sem=q_send.at[0], recv_sem=q_recv.at[other],
            device_id={"chan": other}, device_id_type=MESH,
        ).wait_recv()

    spot = lane_ids((8, 128)) // 16
    for g in range(4):
        wide = [block_recv[8 * g + s].astype(F32) for s in range(8)]
        for u in range(SPAN):
            if u < 8:
                mixed = wide[0][0:8]
                for s in range(1, 8):
                    mixed = jnp.where(spot == (u + s) % 8, wide[s][0:8], mixed)
                if u:
                    mixed = pltpu.roll(mixed, 128 - 16 * u, 1)
            else:
                mixed = None
                for s in range(8):
                    shift = (16 * (s - (u - 8))) % 128
                    moved = pltpu.roll(wide[s][8:16], shift, 1) if shift else wide[s][8:16]
                    mixed = moved if mixed is None else jnp.where(spot == s, moved, mixed)
            lhs[32 + 8 * u : 40 + 8 * u, 128 * g : 128 * (g + 1)] = mixed

    found = None
    for d in range(D2MAX + 1):
        term = jnp.dot(lhs[8 * d : 8 * d + 128, :].astype(BF16), weights[d], preferred_element_type=F32)
        found = term if found is None else found + term
    found = found * (1.0 / math.sqrt(C))
    swap_send[...] = found[0:80]
    swap = to_core(swap_send, swap_recv, s_send, s_recv)
    out_ref[0 : 8 * SPAN, :] = found[32:128]
    out_ref[8 * SPAN : 8 * SPAN_V, :] = jnp.zeros((8 * BOXMAX, ND), F32)
    swap.wait_recv()
    taken = jnp.where(jnp.full((80, ND), sec, jnp.int32) == 0, swap_recv[...], 0.0)
    out_ref[64 : 8 * SPAN_V, :] += taken

    for group in (halves_up, halves_down, direct_up, direct_down, passed_up, passed_down):
        for copy in group:
            copy.wait_send()
    for copy in base_copies + sum(part_copies.values(), []):
        copy.wait_send()
    for copy in chan_copies:
        copy.wait_send()
    rim_copy.wait_send()
    swap.wait_send()


def search(voltages, positions, chan_delays, sub_delays):
    hbm = pl.BlockSpec(memory_space=pltpu.HBM)
    dma = pltpu.SemaphoreType.DMA
    return pl.pallas_call(
        kernel,
        out_shape=pltpu.VMEM((8 * SPAN_V, ND), F32),
        in_specs=[hbm, hbm, hbm, hbm],
        out_specs=pl.BlockSpec(memory_space=pltpu.VMEM),
        scratch_shapes=[
            pltpu.VMEM((8, 128), jnp.int32),
            pltpu.VMEM((CHANS, ND), jnp.int32),
            pltpu.VMEM((2, SPAN, 256, 256), BF16),
            pltpu.VMEM((4, CHUNKS, 512, 256), BF16),
            pltpu.VMEM((CHUNKS, 3, 512, 256), BF16),
            pltpu.VMEM((CHUNKS, 256, 256), BF16),
            pltpu.VMEM((CHUNKS, 256, 256), BF16),
            pltpu.VMEM((4, 2 * NF, 512), BF16),
            pltpu.VMEM((CHUNKS, 2 * NF, 256), F32),
            pltpu.VMEM((NF, SPAN * LOCAL), F32),
            pltpu.VMEM((NF, 128), F32),
            pltpu.VMEM((2, 512, 128), F32),
            pltpu.VMEM((2, 512, 128), F32),
            pltpu.VMEM((NK, SUBCH), jnp.int32),
            pltpu.VMEM((SUBCH, 256), F32),
            pltpu.VMEM(((SPAN + D1MAX) * LOCAL, 256), BF16),
            pltpu.VMEM((D2MAX + 1, 512, ND), BF16),
            pltpu.VMEM((4, 4, 2, 48, 128), F32),
            pltpu.VMEM((4, 4, 2, 48, 128), BF16),
            pltpu.VMEM((4, 3, 2, 48, 128), BF16),
            pltpu.VMEM((8, 4, 16, 128), BF16),
            pltpu.VMEM((CHANS, 16, 128), BF16),
            pltpu.VMEM((160, 512), F32),
            pltpu.VMEM((80, ND), F32),
            pltpu.VMEM((80, ND), F32),
            pltpu.VMEM((4, 32, 256), F32),
            dma((CHUNKS,)),
            dma,
            dma,
            dma,
            dma((6 * CHUNKS,)),
            dma((6 * CHUNKS,)),
            dma,
            dma,
            dma((2,)),
            dma((2,)),
            dma((12,)),
            dma((12,)),
            dma((CHANS,)),
            dma((CHANS,)),
            dma,
            dma,
        ],
        compiler_params=pltpu.CompilerParams(
            collective_id=0, has_side_effects=True, vmem_limit_bytes=60 * 1024 * 1024
        ),
        name="search",
    )(
        jnp.transpose(voltages, (0, 2, 1, 3)),
        positions.reshape(8, 128),
        chan_delays,
        jnp.transpose(sub_delays),
    )


def boxcar_kernel(box_ref, ext_ref, out_ref, held, sems):
    copies = []
    for filter_index in range(NW):
        width_now = box_ref[0, filter_index]
        stride_now = box_ref[1, filter_index]
        gain = lax.rsqrt(jnp.full((8, ND), width_now, jnp.int32).astype(F32))
        summed = ext_ref[0:SPAN]
        for offset in range(1, NW + 1):
            start = jnp.minimum(offset * stride_now, BOXMAX)
            kept = jnp.where(offset < width_now, 1.0, 0.0)
            summed = summed + ext_ref[pl.ds(start, SPAN)] * kept
        held[filter_index] = summed * gain[None]
        copies.append(
            pltpu.make_async_copy(held.at[filter_index], out_ref.at[:, filter_index], sems.at[filter_index])
        )
        copies[-1].start()
    for copy in copies:
        copy.wait()


def boxcar_filter(extended, boxcars):
    filtered = pl.pallas_call(
        boxcar_kernel,
        out_shape=jax.ShapeDtypeStruct((SPAN, NW, 8, ND), F32),
        in_specs=[pl.BlockSpec(memory_space=pltpu.SMEM), pl.BlockSpec(memory_space=pltpu.VMEM)],
        out_specs=pl.BlockSpec(memory_space=pl.ANY),
        scratch_shapes=[pltpu.VMEM((NW, SPAN, 8, ND), F32), pltpu.SemaphoreType.DMA((NW,))],
        compiler_params=pltpu.CompilerParams(vmem_limit_bytes=8 * 1024 * 1024),
        name="boxcar",
    )(jnp.transpose(boxcars), extended)
    return jnp.transpose(filtered, (2, 0, 1, 3))


def per_device(voltages, positions, chan_delays, sub_delays, boxcars):
    extended = search(voltages, positions, chan_delays, sub_delays)
    return boxcar_filter(extended.reshape(SPAN_V, 8, ND), boxcars)


def solution(mesh):
    return jax.shard_map(
        per_device,
        mesh=mesh,
        in_specs=(P(None, "feed", "section", "chan"), P(), P(), P(), P()),
        out_specs=P(("chan", "feed"), "section", None, None),
        check_vma=False,
    )
```

```python
import math

import jax
import jax.numpy as jnp
from jax import lax
from jax.experimental import pallas as pl
from jax.experimental.pallas import tpu as pltpu
from jax.sharding import PartitionSpec as P

NF = 1024
C = 8192
NK = 16
ND = 256
NW = 3
D1MAX = 2
D2MAX = 4
BOXMAX = 6
TT = 24
SUBCH = 256
EPSILON = 1e-05

SPAN = 12
LOCAL = 64
CHANS = 32
FEEDS = 4
CHUNKS = 3
SPAN_V = SPAN + BOXMAX
F32 = jnp.float32
BF16 = jnp.bfloat16
MESH = pl.DeviceIdType.MESH


def lane_ids(shape):
    return lax.broadcasted_iota(jnp.int32, shape, len(shape) - 1)


def row_ids(shape):
    return lax.broadcasted_iota(jnp.int32, shape, len(shape) - 2)


def kernel(
    v_ref, pos_any, cd_ref, sd_any, out_ref,
    pos_ref, sd_ref, vbuf, packed, arrived, relay_up, relay_down, table, acc, power,
    rim, base_own, base_other, cdbuf, delay_t, chooser, weights,
    part_own, part_send, part_recv, block_send, block_recv, lhs, swap_send, swap_recv, trig,
    v_sem, cd_sem, pos_sem, sd_sem, a_send, a_recv, r_send, r_recv, b_send, b_recv, p_send, p_recv, q_send, q_recv, s_send, s_recv, word,
):
    sec = lax.axis_index("section")
    ch = lax.axis_index("chan")
    fd = lax.axis_index("feed")
    zed, ex = lax.div(ch, 4), lax.rem(ch, 4)
    up, down, far = lax.rem(fd + 1, 4), lax.rem(fd + 3, 4), lax.rem(fd + 2, 4)

    barrier = pltpu.get_barrier_semaphore()
    beside = [lax.rem(zed + n, 8) * 4 + ex for n in (1, 7)]
    across = [zed * 4 + lax.rem(ex + n, 4) for n in (1, 3)]
    pl.semaphore_signal(barrier, inc=1, device_id={"section": 1 - sec}, device_id_type=MESH)
    for other in (far, up, down):
        pl.semaphore_signal(barrier, inc=1, device_id={"feed": other}, device_id_type=MESH)
    for other in beside + across:
        pl.semaphore_signal(barrier, inc=1, device_id={"chan": other}, device_id_type=MESH)

    loads = []
    for j in range(CHUNKS):
        loads.append(
            pltpu.make_async_copy(v_ref.at[:, pl.ds(4 * j, 4)], vbuf.at[:, pl.ds(4 * j, 4)], v_sem.at[j])
        )
        loads[j].start()
    first = pl.multiple_of(ch * SUBCH, SUBCH)
    cd_load = pltpu.make_async_copy(cd_ref.at[:, pl.ds(first, SUBCH)], cdbuf, cd_sem)
    cd_load.start()
    pos_load = pltpu.make_async_copy(pos_any, pos_ref, pos_sem)
    pos_load.start()
    sd_load = pltpu.make_async_copy(sd_any, sd_ref, sd_sem)
    sd_load.start()

    low_half = lane_ids((256, 128)) < LOCAL
    for j in range(CHUNKS):
        loads[j].wait()
        for part in range(2):
            for pair in range(2):
                for tile in range(2):
                    lanes = pl.ds(128 * tile, 128)
                    a = vbuf[part, 4 * j + 2 * pair, :, lanes]
                    b = vbuf[part, 4 * j + 2 * pair + 1, :, lanes]
                    even = jnp.where(low_half, a, pltpu.roll(b, LOCAL, 1))
                    odd = jnp.where(low_half, pltpu.roll(a, LOCAL, 1), b)
                    rows = pl.ds(256 * part, 256)
                    packed[2 * tile, j, rows, pl.ds(128 * pair, 128)] = even
                    packed[2 * tile + 1, j, rows, pl.ds(128 * pair, 128)] = odd

    pl.semaphore_wait(barrier, 8)

    def to_feed(src, dst, sems, index, other):
        copy = pltpu.make_async_remote_copy(
            src_ref=src, dst_ref=dst, send_sem=sems[0].at[index], recv_sem=sems[1].at[index],
            device_id={"feed": other}, device_id_type=MESH,
        )
        copy.start()
        return copy

    a_sems = (a_send, a_recv)
    halves_up, halves_down, direct_up, direct_down, passed_up, passed_down = [], [], [], [], [], []
    re_rows, im_rows = pl.ds(0, 256), pl.ds(256, 256)
    for j in range(CHUNKS):
        halves_up.append(to_feed(packed.at[far, j, re_rows], relay_up.at[j], a_sems, 6 * j, up))
        halves_down.append(to_feed(packed.at[far, j, im_rows], relay_down.at[j], a_sems, 6 * j + 1, down))
    for j in range(CHUNKS):
        direct_up.append(to_feed(packed.at[up, j], arrived.at[j, 0], a_sems, 6 * j + 2, up))
        direct_down.append(to_feed(packed.at[down, j], arrived.at[j, 1], a_sems, 6 * j + 3, down))

    def tell(n, others):
        if n:
            pl.semaphore_wait(word.at[n - 1], 2)
        for other in others:
            pl.semaphore_signal(word.at[n], inc=1, device_id={"chan": other}, device_id_type=MESH)

    tell(0, across)

    step = 2.0 * math.pi / NF
    pos_load.wait()
    for q, owner in enumerate((fd, down, up, far)):
        place = jnp.concatenate(
            [pos_ref[pl.ds(2 * owner, 1), :], pos_ref[pl.ds(2 * owner + 1, 1), :]], axis=1
        )
        ids = row_ids((32, 256))
        fine = ((ids * place) & (NF - 1)).astype(F32) * step
        coarse = ((ids * 32 * place) & (NF - 1)).astype(F32) * step
        trig[0] = jnp.cos(coarse)
        trig[1] = jnp.sin(coarse)
        trig[2] = jnp.cos(fine)
        trig[3] = jnp.sin(fine)

        @pl.loop(0, CHANS // 2)
        def _(i):
            hop = lax.div(i, 2)
            pair = lax.rem(i, 2)
            chan = lax.rem(zed + hop + 3, 8) * 4 + 2 * pair
            base = lax.div(hop, 2) * 256 + lax.rem(hop, 2) * 32 + pair * 16
            cos_c = jnp.concatenate(
                [jnp.broadcast_to(trig[0, pl.ds(chan + n, 1), :], (8, 256)) for n in range(2)], axis=0
            )
            sin_c = jnp.concatenate(
                [jnp.broadcast_to(trig[1, pl.ds(chan + n, 1), :], (8, 256)) for n in range(2)], axis=0
            )
            for f in range(FEEDS):
                cos_f = jnp.concatenate([trig[2, 8 * f : 8 * f + 8, :]] * 2, axis=0)
                sin_f = jnp.concatenate([trig[3, 8 * f : 8 * f + 8, :]] * 2, axis=0)
                cosine = (cos_c * cos_f - sin_c * sin_f).astype(BF16)
                sine = sin_c * cos_f + cos_c * sin_f
                upper = pl.ds(pl.multiple_of(64 * f + base, 16), 16)
                lower = pl.ds(pl.multiple_of(NF + 64 * f + base, 16), 16)
                table[q, upper, 0:256] = cosine
                table[q, upper, 256:512] = sine.astype(BF16)
                table[q, lower, 0:256] = (-sine).astype(BF16)
                table[q, lower, 256:512] = cosine

    def block_dot(q, rows, right):
        return jnp.dot(table[q, rows, :], right, preferred_element_type=F32)

    for j in range(CHUNKS):
        @pl.loop(0, 4)
        def _(m):
            rows = pl.ds(pl.multiple_of(512 * m, 512), 512)
            acc[j, rows, :] = block_dot(0, rows, packed[fd, j])

    tell(1, beside)
    for j in range(CHUNKS):
        halves_up[j].wait_recv()
        passed_up.append(to_feed(relay_up.at[j], arrived.at[j, 2, re_rows], a_sems, 6 * j + 4, up))
        halves_down[j].wait_recv()
        passed_down.append(to_feed(relay_down.at[j], arrived.at[j, 2, im_rows], a_sems, 6 * j + 5, down))

    tell(2, beside)

    cd_load.wait()
    one_k = (row_ids((NK, 256)) == (lane_ids((NK, 256)) & (NK - 1))).astype(BF16)
    delay_t[...] = lax.dot_general(
        cdbuf[...].astype(F32).astype(BF16), one_k, (((0,), (0,)), ((), ())), preferred_element_type=F32
    )
    mine = delay_t[pl.ds(pl.multiple_of(fd * LOCAL, LOCAL), LOCAL), :]
    lanes = lane_ids((LOCAL, 256))
    spot = (lanes & 127) // 16
    early = (spot + 8 - lax.rem(ch, 8)) & 7
    u_of = jnp.where(lanes < 128, early, 8 + (spot & 3)).astype(F32)
    for t in range(SPAN + D1MAX):
        hit = (u_of + mine) == float(t)
        if t >= SPAN:
            hit = hit & (jnp.full((LOCAL, 256), sec, jnp.int32) == 0)
        chooser[LOCAL * t : LOCAL * (t + 1), :] = jnp.where(hit, 1.0, 0.0).astype(BF16)

    sd_load.wait()
    own_k = row_ids((NK, ND)) == lane_ids((NK, ND)) * NK // ND

    @pl.loop(0, CHANS)
    def _(s):
        delay = jnp.broadcast_to(sd_ref[pl.ds(s, 1), :], (NK, ND))
        rows = pl.ds(pl.multiple_of(NK * s, NK), NK)
        for d in range(D2MAX + 1):
            weights[d, rows, :] = jnp.where(own_k & (delay == d), 1.0, 0.0).astype(BF16)

    tell(3, beside)
    for j in range(CHUNKS):
        direct_up[j].wait_recv()
        direct_down[j].wait_recv()

        @pl.loop(0, 4)
        def _(m):
            rows = pl.ds(pl.multiple_of(512 * m, 512), 512)
            acc[j, rows, :] += block_dot(1, rows, arrived[j, 0]) + block_dot(2, rows, arrived[j, 1])

    tell(4, beside)
    pl.semaphore_wait(word.at[4], 2)

    def beam_power(j, m):
        rows = pl.ds(pl.multiple_of(512 * m, 512), 512)
        lower = pl.ds(pl.multiple_of(NF + 512 * m, 512), 512)
        right = arrived[j, 2]
        re = acc[j, rows, :] + block_dot(3, rows, right)
        im = acc[j, lower, :] + block_dot(3, lower, right)
        power[rows, 256 * j : 256 * (j + 1)] = re * re + im * im

    def to_core(src, dst, send_sem, recv_sem):
        copy = pltpu.make_async_remote_copy(
            src_ref=src, dst_ref=dst, send_sem=send_sem, recv_sem=recv_sem,
            device_id={"section": 1 - sec}, device_id_type=MESH,
        )
        copy.start()
        return copy

    rim_copy = None
    for j in range(CHUNKS - 1):
        passed_up[j].wait_recv()
        passed_down[j].wait_recv()

        @pl.loop(0, 2)
        def _(m):
            beam_power(j, m)

        if j == 0:
            rim_copy = to_core(power.at[:, pl.ds(0, 128)], rim, r_send, r_recv)

    passed_up[CHUNKS - 1].wait_recv()
    passed_down[CHUNKS - 1].wait_recv()
    base_copies = []
    for h in range(2):
        beam_power(CHUNKS - 1, h)
        rows = pl.ds(512 * h, 512)
        total = power[rows, 0:128]
        for tile in range(1, 6):
            total = total + power[rows, 128 * tile : 128 * (tile + 1)]
        base_own[h] = total + pltpu.roll(total, LOCAL, 1)
        base_copies.append(to_core(base_own.at[h], base_other.at[h], b_send.at[h], b_recv.at[h]))

    rim_copy.wait_recv()
    low_lanes = lane_ids((4, 2, 2, 8, 128)) < LOCAL
    part_copies = {}
    turns = (0, 1, 3, 2)
    for q in turns:
        h = q // 2
        if q in (0, 3):
            base_copies[h].wait_recv()
        within = pl.ds(256 * (q % 2), 256)
        rows = pl.ds(256 * q, 256)
        scale = 1.0 / ((base_own[h, within] + base_other[h, within]) * (1.0 / TT) + EPSILON)
        tiles = [power[rows, 128 * tile : 128 * (tile + 1)] * scale - 1.0 for tile in range(6)]
        tiles.append(rim[rows, :] * scale - 1.0)
        summed = None
        for tile in range(4):
            normed = jnp.concatenate(tiles[2 * tile : 2 * tile + 2], axis=1)
            high = normed.astype(BF16)
            low = (normed - high.astype(F32)).astype(BF16)
            chosen = chooser[256 * tile : 256 * tile + normed.shape[1], :]
            term = jnp.dot(jnp.concatenate([high, low], axis=0), chosen, preferred_element_type=F32)
            summed = term if summed is None else summed + term
        summed = summed[0:256] + summed[256:512]
        early = summed[:, 0:128].reshape(4, 2, 32, 128)
        late = summed[:, 128:256].reshape(4, 2, 2, 2, 8, 128)
        late = jnp.where(low_lanes, late[:, :, :, 0], late[:, :, :, 1]).reshape(4, 2, 16, 128)
        blocks = jnp.concatenate([early, late], axis=2)
        part_own[q] = blocks
        part_send[q] = blocks.astype(BF16)
        part_copies[q] = [
            to_feed(part_send.at[q, f], part_recv.at[q, n], (p_send, p_recv), 3 * q + n, f)
            for n, f in enumerate((far, up, down))
        ]

    lhs[0:32, :] = jnp.zeros((32, 512), F32)
    lhs[128:160, :] = jnp.zeros((32, 512), F32)

    chan_copies = []
    for q in turns:
        total = part_own[q, fd]
        for n in range(3):
            part_copies[q][n].wait_recv()
            total = total + part_recv[q, n].astype(F32)
        for x in range(4):
            late = total[:, 32 + 8 * (x // 2) : 40 + 8 * (x // 2)].reshape(16, 128)
            if x % 2:
                late = pltpu.roll(late, LOCAL, 1)
            block = jnp.concatenate([total[:, 8 * x : 8 * x + 8], late.reshape(2, 8, 128)], axis=1)
            block_send[2 * q : 2 * q + 2, x] = block.astype(BF16)
        for a in range(2):
            spot = 2 * q + a
            hop = (spot + 3) % 8
            for i in ((2, 1, 3) if hop == 0 else (2, 1, 3, 0)):
                x = lax.rem(ex + i, 4)
                other = lax.rem(zed + hop, 8) * 4 + x
                copy = pltpu.make_async_remote_copy(
                    src_ref=block_send.at[spot, x], dst_ref=block_recv.at[ch],
                    send_sem=q_send.at[4 * spot + i], recv_sem=q_recv.at[ch],
                    device_id={"chan": other}, device_id_type=MESH,
                )
                copy.start()
                chan_copies.append(copy)

    block_recv[ch] = block_send[5, ex]

    @pl.loop(1, CHANS)
    def _(i):
        other = lax.rem(ch + i, CHANS)
        pltpu.make_async_remote_copy(
            src_ref=block_send.at[0, 0], dst_ref=block_recv.at[other],
            send_sem=q_send.at[0], recv_sem=q_recv.at[other],
            device_id={"chan": other}, device_id_type=MESH,
        ).wait_recv()

    spot = lane_ids((8, 128)) // 16
    for g in range(4):
        wide = [block_recv[8 * g + s].astype(F32) for s in range(8)]
        for u in range(SPAN):
            if u < 8:
                mixed = wide[0][0:8]
                for s in range(1, 8):
                    mixed = jnp.where(spot == (u + s) % 8, wide[s][0:8], mixed)
                if u:
                    mixed = pltpu.roll(mixed, 128 - 16 * u, 1)
            else:
                mixed = None
                for s in range(8):
                    shift = (16 * (s - (u - 8))) % 128
                    moved = pltpu.roll(wide[s][8:16], shift, 1) if shift else wide[s][8:16]
                    mixed = moved if mixed is None else jnp.where(spot == s, moved, mixed)
            lhs[32 + 8 * u : 40 + 8 * u, 128 * g : 128 * (g + 1)] = mixed

    found = None
    for d in range(D2MAX + 1):
        term = jnp.dot(lhs[8 * d : 8 * d + 128, :].astype(BF16), weights[d], preferred_element_type=F32)
        found = term if found is None else found + term
    found = found * (1.0 / math.sqrt(C))
    swap_send[...] = found[0:80]
    swap = to_core(swap_send, swap_recv, s_send, s_recv)
    out_ref[0 : 8 * SPAN, :] = found[32:128]
    out_ref[8 * SPAN : 8 * SPAN_V, :] = jnp.zeros((8 * BOXMAX, ND), F32)
    swap.wait_recv()
    taken = jnp.where(jnp.full((80, ND), sec, jnp.int32) == 0, swap_recv[...], 0.0)
    out_ref[64 : 8 * SPAN_V, :] += taken

    for group in (halves_up, halves_down, direct_up, direct_down, passed_up, passed_down):
        for copy in group:
            copy.wait_send()
    for copy in base_copies + sum(part_copies.values(), []):
        copy.wait_send()
    for copy in chan_copies:
        copy.wait_send()
    rim_copy.wait_send()
    swap.wait_send()


def search(voltages, positions, chan_delays, sub_delays):
    hbm = pl.BlockSpec(memory_space=pltpu.HBM)
    dma = pltpu.SemaphoreType.DMA
    return pl.pallas_call(
        kernel,
        out_shape=pltpu.VMEM((8 * SPAN_V, ND), F32),
        in_specs=[hbm, hbm, hbm, hbm],
        out_specs=pl.BlockSpec(memory_space=pltpu.VMEM),
        scratch_shapes=[
            pltpu.VMEM((8, 128), jnp.int32),
            pltpu.VMEM((CHANS, ND), jnp.int32),
            pltpu.VMEM((2, SPAN, 256, 256), BF16),
            pltpu.VMEM((4, CHUNKS, 512, 256), BF16),
            pltpu.VMEM((CHUNKS, 3, 512, 256), BF16),
            pltpu.VMEM((CHUNKS, 256, 256), BF16),
            pltpu.VMEM((CHUNKS, 256, 256), BF16),
            pltpu.VMEM((4, 2 * NF, 512), BF16),
            pltpu.VMEM((CHUNKS, 2 * NF, 256), F32),
            pltpu.VMEM((NF, SPAN * LOCAL), F32),
            pltpu.VMEM((NF, 128), F32),
            pltpu.VMEM((2, 512, 128), F32),
            pltpu.VMEM((2, 512, 128), F32),
            pltpu.VMEM((NK, SUBCH), jnp.int32),
            pltpu.VMEM((SUBCH, 256), F32),
            pltpu.VMEM(((SPAN + D1MAX) * LOCAL, 256), BF16),
            pltpu.VMEM((D2MAX + 1, 512, ND), BF16),
            pltpu.VMEM((4, 4, 2, 48, 128), F32),
            pltpu.VMEM((4, 4, 2, 48, 128), BF16),
            pltpu.VMEM((4, 3, 2, 48, 128), BF16),
            pltpu.VMEM((8, 4, 16, 128), BF16),
            pltpu.VMEM((CHANS, 16, 128), BF16),
            pltpu.VMEM((160, 512), F32),
            pltpu.VMEM((80, ND), F32),
            pltpu.VMEM((80, ND), F32),
            pltpu.VMEM((4, 32, 256), F32),
            dma((CHUNKS,)),
            dma,
            dma,
            dma,
            dma((6 * CHUNKS,)),
            dma((6 * CHUNKS,)),
            dma,
            dma,
            dma((2,)),
            dma((2,)),
            dma((12,)),
            dma((12,)),
            dma((CHANS,)),
            dma((CHANS,)),
            dma,
            dma,
            pltpu.SemaphoreType.REGULAR((5,)),
        ],
        compiler_params=pltpu.CompilerParams(
            collective_id=0, has_side_effects=True, vmem_limit_bytes=60 * 1024 * 1024
        ),
        name="search",
    )(
        jnp.transpose(voltages, (0, 2, 1, 3)),
        positions.reshape(8, 128),
        chan_delays,
        jnp.transpose(sub_delays),
    )


def boxcar_kernel(box_ref, ext_ref, out_ref, held, sems):
    copies = []
    for filter_index in range(NW):
        width_now = box_ref[0, filter_index]
        stride_now = box_ref[1, filter_index]
        gain = lax.rsqrt(jnp.full((8, ND), width_now, jnp.int32).astype(F32))
        summed = ext_ref[0:SPAN]
        for offset in range(1, NW + 1):
            start = jnp.minimum(offset * stride_now, BOXMAX)
            kept = jnp.where(offset < width_now, 1.0, 0.0)
            summed = summed + ext_ref[pl.ds(start, SPAN)] * kept
        held[filter_index] = summed * gain[None]
        copies.append(
            pltpu.make_async_copy(held.at[filter_index], out_ref.at[:, filter_index], sems.at[filter_index])
        )
        copies[-1].start()
    for copy in copies:
        copy.wait()


def boxcar_filter(extended, boxcars):
    filtered = pl.pallas_call(
        boxcar_kernel,
        out_shape=jax.ShapeDtypeStruct((SPAN, NW, 8, ND), F32),
        in_specs=[pl.BlockSpec(memory_space=pltpu.SMEM), pl.BlockSpec(memory_space=pltpu.VMEM)],
        out_specs=pl.BlockSpec(memory_space=pl.ANY),
        scratch_shapes=[pltpu.VMEM((NW, SPAN, 8, ND), F32), pltpu.SemaphoreType.DMA((NW,))],
        compiler_params=pltpu.CompilerParams(vmem_limit_bytes=8 * 1024 * 1024),
        name="boxcar",
    )(jnp.transpose(boxcars), extended)
    return jnp.transpose(filtered, (2, 0, 1, 3))


def per_device(voltages, positions, chan_delays, sub_delays, boxcars):
    extended = search(voltages, positions, chan_delays, sub_delays)
    return boxcar_filter(extended.reshape(SPAN_V, 8, ND), boxcars)


def solution(mesh):
    return jax.shard_map(
        per_device,
        mesh=mesh,
        in_specs=(P(None, "feed", "section", "chan"), P(), P(), P(), P()),
        out_specs=P(("chan", "feed"), "section", None, None),
        check_vma=False,
    )
```

```python
import math

import jax
import jax.numpy as jnp
from jax import lax
from jax.experimental import pallas as pl
from jax.experimental.pallas import tpu as pltpu
from jax.sharding import PartitionSpec as P

NF = 1024
C = 8192
NK = 16
ND = 256
NW = 3
D1MAX = 2
D2MAX = 4
BOXMAX = 6
TT = 24
SUBCH = 256
EPSILON = 1e-05

SPAN = 12
LOCAL = 64
CHANS = 32
FEEDS = 4
CHUNKS = 3
SPAN_V = SPAN + BOXMAX
F32 = jnp.float32
BF16 = jnp.bfloat16
MESH = pl.DeviceIdType.MESH


def lane_ids(shape):
    return lax.broadcasted_iota(jnp.int32, shape, len(shape) - 1)


def row_ids(shape):
    return lax.broadcasted_iota(jnp.int32, shape, len(shape) - 2)


def kernel(
    v_ref, pos_any, cd_ref, sd_any, out_ref,
    pos_ref, sd_ref, vbuf, packed, arrived, relay_up, relay_down, table, acc, power,
    rim, base_own, base_other, cdbuf, delay_t, chooser, weights,
    part_own, part_send, part_recv, block_send, block_recv, lhs, swap_send, swap_recv, trig,
    v_sem, cd_sem, pos_sem, sd_sem, a_send, a_recv, r_send, r_recv, b_send, b_recv, p_send, p_recv, q_send, q_recv, s_send, s_recv, word,
):
    sec = lax.axis_index("section")
    ch = lax.axis_index("chan")
    fd = lax.axis_index("feed")
    zed, ex = lax.div(ch, 4), lax.rem(ch, 4)
    up, down, far = lax.rem(fd + 1, 4), lax.rem(fd + 3, 4), lax.rem(fd + 2, 4)

    barrier = pltpu.get_barrier_semaphore()
    beside = [lax.rem(zed + n, 8) * 4 + ex for n in (1, 7)]
    across = [zed * 4 + lax.rem(ex + n, 4) for n in (1, 3)]
    pl.semaphore_signal(barrier, inc=1, device_id={"section": 1 - sec}, device_id_type=MESH)
    for other in (far, up, down):
        pl.semaphore_signal(barrier, inc=1, device_id={"feed": other}, device_id_type=MESH)
    for other in beside + across:
        pl.semaphore_signal(barrier, inc=1, device_id={"chan": other}, device_id_type=MESH)

    loads = []
    for j in range(CHUNKS):
        loads.append(
            pltpu.make_async_copy(v_ref.at[:, pl.ds(4 * j, 4)], vbuf.at[:, pl.ds(4 * j, 4)], v_sem.at[j])
        )
        loads[j].start()
    first = pl.multiple_of(ch * SUBCH, SUBCH)
    cd_load = pltpu.make_async_copy(cd_ref.at[:, pl.ds(first, SUBCH)], cdbuf, cd_sem)
    cd_load.start()
    pos_load = pltpu.make_async_copy(pos_any, pos_ref, pos_sem)
    pos_load.start()
    sd_load = pltpu.make_async_copy(sd_any, sd_ref, sd_sem)
    sd_load.start()

    def to_feed(src, dst, sems, index, other):
        copy = pltpu.make_async_remote_copy(
            src_ref=src, dst_ref=dst, send_sem=sems[0].at[index], recv_sem=sems[1].at[index],
            device_id={"feed": other}, device_id_type=MESH,
        )
        copy.start()
        return copy

    a_sems = (a_send, a_recv)
    halves_up, halves_down, direct_up, direct_down, passed_up, passed_down = [], [], [], [], [], []
    re_rows, im_rows = pl.ds(0, 256), pl.ds(256, 256)
    low_half = lane_ids((256, 128)) < LOCAL
    for j in range(CHUNKS):
        loads[j].wait()
        for part in range(2):
            for pair in range(2):
                for tile in range(2):
                    lanes = pl.ds(128 * tile, 128)
                    a = vbuf[part, 4 * j + 2 * pair, :, lanes]
                    b = vbuf[part, 4 * j + 2 * pair + 1, :, lanes]
                    even = jnp.where(low_half, a, pltpu.roll(b, LOCAL, 1))
                    odd = jnp.where(low_half, pltpu.roll(a, LOCAL, 1), b)
                    rows = pl.ds(256 * part, 256)
                    packed[2 * tile, j, rows, pl.ds(128 * pair, 128)] = even
                    packed[2 * tile + 1, j, rows, pl.ds(128 * pair, 128)] = odd
        if j == 0:
            pl.semaphore_wait(barrier, 8)
        halves_up.append(to_feed(packed.at[far, j, re_rows], relay_up.at[j], a_sems, 6 * j, up))
        halves_down.append(to_feed(packed.at[far, j, im_rows], relay_down.at[j], a_sems, 6 * j + 1, down))
    for j in range(CHUNKS):
        direct_up.append(to_feed(packed.at[up, j], arrived.at[j, 0], a_sems, 6 * j + 2, up))
        direct_down.append(to_feed(packed.at[down, j], arrived.at[j, 1], a_sems, 6 * j + 3, down))

    def tell(n, others):
        if n:
            pl.semaphore_wait(word.at[n - 1], 2)
        for other in others:
            pl.semaphore_signal(word.at[n], inc=1, device_id={"chan": other}, device_id_type=MESH)

    tell(0, across)

    step = 2.0 * math.pi / NF
    pos_load.wait()
    for q, owner in enumerate((fd, down, up, far)):
        place = jnp.concatenate(
            [pos_ref[pl.ds(2 * owner, 1), :], pos_ref[pl.ds(2 * owner + 1, 1), :]], axis=1
        )
        ids = row_ids((32, 256))
        fine = ((ids * place) & (NF - 1)).astype(F32) * step
        coarse = ((ids * 32 * place) & (NF - 1)).astype(F32) * step
        trig[0] = jnp.cos(coarse)
        trig[1] = jnp.sin(coarse)
        trig[2] = jnp.cos(fine)
        trig[3] = jnp.sin(fine)

        @pl.loop(0, CHANS // 2)
        def _(i):
            hop = lax.div(i, 2)
            pair = lax.rem(i, 2)
            chan = lax.rem(zed + hop + 3, 8) * 4 + 2 * pair
            base = lax.div(hop, 2) * 256 + lax.rem(hop, 2) * 32 + pair * 16
            cos_c = jnp.concatenate(
                [jnp.broadcast_to(trig[0, pl.ds(chan + n, 1), :], (8, 256)) for n in range(2)], axis=0
            )
            sin_c = jnp.concatenate(
                [jnp.broadcast_to(trig[1, pl.ds(chan + n, 1), :], (8, 256)) for n in range(2)], axis=0
            )
            for f in range(FEEDS):
                cos_f = jnp.concatenate([trig[2, 8 * f : 8 * f + 8, :]] * 2, axis=0)
                sin_f = jnp.concatenate([trig[3, 8 * f : 8 * f + 8, :]] * 2, axis=0)
                cosine = (cos_c * cos_f - sin_c * sin_f).astype(BF16)
                sine = sin_c * cos_f + cos_c * sin_f
                upper = pl.ds(pl.multiple_of(64 * f + base, 16), 16)
                lower = pl.ds(pl.multiple_of(NF + 64 * f + base, 16), 16)
                table[q, upper, 0:256] = cosine
                table[q, upper, 256:512] = sine.astype(BF16)
                table[q, lower, 0:256] = (-sine).astype(BF16)
                table[q, lower, 256:512] = cosine

    def block_dot(q, rows, right):
        return jnp.dot(table[q, rows, :], right, preferred_element_type=F32)

    for j in range(CHUNKS):
        @pl.loop(0, 4)
        def _(m):
            rows = pl.ds(pl.multiple_of(512 * m, 512), 512)
            acc[j, rows, :] = block_dot(0, rows, packed[fd, j])

    tell(1, beside)
    for j in range(CHUNKS):
        halves_up[j].wait_recv()
        passed_up.append(to_feed(relay_up.at[j], arrived.at[j, 2, re_rows], a_sems, 6 * j + 4, up))
        halves_down[j].wait_recv()
        passed_down.append(to_feed(relay_down.at[j], arrived.at[j, 2, im_rows], a_sems, 6 * j + 5, down))

    tell(2, beside)

    cd_load.wait()
    one_k = (row_ids((NK, 256)) == (lane_ids((NK, 256)) & (NK - 1))).astype(BF16)
    delay_t[...] = lax.dot_general(
        cdbuf[...].astype(F32).astype(BF16), one_k, (((0,), (0,)), ((), ())), preferred_element_type=F32
    )
    mine = delay_t[pl.ds(pl.multiple_of(fd * LOCAL, LOCAL), LOCAL), :]
    lanes = lane_ids((LOCAL, 256))
    spot = (lanes & 127) // 16
    early = (spot + 8 - lax.rem(ch, 8)) & 7
    u_of = jnp.where(lanes < 128, early, 8 + (spot & 3)).astype(F32)
    for t in range(SPAN + D1MAX):
        hit = (u_of + mine) == float(t)
        if t >= SPAN:
            hit = hit & (jnp.full((LOCAL, 256), sec, jnp.int32) == 0)
        chooser[LOCAL * t : LOCAL * (t + 1), :] = jnp.where(hit, 1.0, 0.0).astype(BF16)

    sd_load.wait()
    own_k = row_ids((NK, ND)) == lane_ids((NK, ND)) * NK // ND

    @pl.loop(0, CHANS)
    def _(s):
        delay = jnp.broadcast_to(sd_ref[pl.ds(s, 1), :], (NK, ND))
        rows = pl.ds(pl.multiple_of(NK * s, NK), NK)
        for d in range(D2MAX + 1):
            weights[d, rows, :] = jnp.where(own_k & (delay == d), 1.0, 0.0).astype(BF16)

    tell(3, beside)
    for j in range(CHUNKS):
        direct_up[j].wait_recv()
        direct_down[j].wait_recv()

        @pl.loop(0, 4)
        def _(m):
            rows = pl.ds(pl.multiple_of(512 * m, 512), 512)
            acc[j, rows, :] += block_dot(1, rows, arrived[j, 0]) + block_dot(2, rows, arrived[j, 1])

    tell(4, beside)
    pl.semaphore_wait(word.at[4], 2)

    def beam_power(j, m):
        rows = pl.ds(pl.multiple_of(512 * m, 512), 512)
        lower = pl.ds(pl.multiple_of(NF + 512 * m, 512), 512)
        right = arrived[j, 2]
        re = acc[j, rows, :] + block_dot(3, rows, right)
        im = acc[j, lower, :] + block_dot(3, lower, right)
        power[rows, 256 * j : 256 * (j + 1)] = re * re + im * im

    def to_core(src, dst, send_sem, recv_sem):
        copy = pltpu.make_async_remote_copy(
            src_ref=src, dst_ref=dst, send_sem=send_sem, recv_sem=recv_sem,
            device_id={"section": 1 - sec}, device_id_type=MESH,
        )
        copy.start()
        return copy

    rim_copy = None
    for j in range(CHUNKS - 1):
        passed_up[j].wait_recv()
        passed_down[j].wait_recv()

        @pl.loop(0, 2)
        def _(m):
            beam_power(j, m)

        if j == 0:
            rim_copy = to_core(power.at[:, pl.ds(0, 128)], rim, r_send, r_recv)

    passed_up[CHUNKS - 1].wait_recv()
    passed_down[CHUNKS - 1].wait_recv()
    base_copies = []
    for h in range(2):
        beam_power(CHUNKS - 1, h)
        rows = pl.ds(512 * h, 512)
        total = power[rows, 0:128]
        for tile in range(1, 6):
            total = total + power[rows, 128 * tile : 128 * (tile + 1)]
        base_own[h] = total + pltpu.roll(total, LOCAL, 1)
        base_copies.append(to_core(base_own.at[h], base_other.at[h], b_send.at[h], b_recv.at[h]))

    rim_copy.wait_recv()
    low_lanes = lane_ids((4, 2, 2, 8, 128)) < LOCAL
    part_copies = {}
    turns = (0, 1, 3, 2)
    for q in turns:
        h = q // 2
        if q in (0, 3):
            base_copies[h].wait_recv()
        within = pl.ds(256 * (q % 2), 256)
        rows = pl.ds(256 * q, 256)
        scale = 1.0 / ((base_own[h, within] + base_other[h, within]) * (1.0 / TT) + EPSILON)
        tiles = [power[rows, 128 * tile : 128 * (tile + 1)] * scale - 1.0 for tile in range(6)]
        tiles.append(rim[rows, :] * scale - 1.0)
        summed = None
        for tile in range(4):
            normed = jnp.concatenate(tiles[2 * tile : 2 * tile + 2], axis=1)
            high = normed.astype(BF16)
            low = (normed - high.astype(F32)).astype(BF16)
            chosen = chooser[256 * tile : 256 * tile + normed.shape[1], :]
            term = jnp.dot(jnp.concatenate([high, low], axis=0), chosen, preferred_element_type=F32)
            summed = term if summed is None else summed + term
        summed = summed[0:256] + summed[256:512]
        early = summed[:, 0:128].reshape(4, 2, 32, 128)
        late = summed[:, 128:256].reshape(4, 2, 2, 2, 8, 128)
        late = jnp.where(low_lanes, late[:, :, :, 0], late[:, :, :, 1]).reshape(4, 2, 16, 128)
        blocks = jnp.concatenate([early, late], axis=2)
        part_own[q] = blocks
        part_send[q] = blocks.astype(BF16)
        part_copies[q] = [
            to_feed(part_send.at[q, f], part_recv.at[q, n], (p_send, p_recv), 3 * q + n, f)
            for n, f in enumerate((far, up, down))
        ]

    lhs[0:32, :] = jnp.zeros((32, 512), F32)
    lhs[128:160, :] = jnp.zeros((32, 512), F32)

    chan_copies = []
    for q in turns:
        total = part_own[q, fd]
        for n in range(3):
            part_copies[q][n].wait_recv()
            total = total + part_recv[q, n].astype(F32)
        for x in range(4):
            late = total[:, 32 + 8 * (x // 2) : 40 + 8 * (x // 2)].reshape(16, 128)
            if x % 2:
                late = pltpu.roll(late, LOCAL, 1)
            block = jnp.concatenate([total[:, 8 * x : 8 * x + 8], late.reshape(2, 8, 128)], axis=1)
            block_send[2 * q : 2 * q + 2, x] = block.astype(BF16)
        for a in range(2):
            spot = 2 * q + a
            hop = (spot + 3) % 8
            for i in ((2, 1, 3) if hop == 0 else (2, 1, 3, 0)):
                x = lax.rem(ex + i, 4)
                other = lax.rem(zed + hop, 8) * 4 + x
                copy = pltpu.make_async_remote_copy(
                    src_ref=block_send.at[spot, x], dst_ref=block_recv.at[ch],
                    send_sem=q_send.at[4 * spot + i], recv_sem=q_recv.at[ch],
                    device_id={"chan": other}, device_id_type=MESH,
                )
                copy.start()
                chan_copies.append(copy)

    block_recv[ch] = block_send[5, ex]

    @pl.loop(1, CHANS)
    def _(i):
        other = lax.rem(ch + i, CHANS)
        pltpu.make_async_remote_copy(
            src_ref=block_send.at[0, 0], dst_ref=block_recv.at[other],
            send_sem=q_send.at[0], recv_sem=q_recv.at[other],
            device_id={"chan": other}, device_id_type=MESH,
        ).wait_recv()

    spot = lane_ids((8, 128)) // 16
    for g in range(4):
        wide = [block_recv[8 * g + s].astype(F32) for s in range(8)]
        for u in range(SPAN):
            if u < 8:
                mixed = wide[0][0:8]
                for s in range(1, 8):
                    mixed = jnp.where(spot == (u + s) % 8, wide[s][0:8], mixed)
                if u:
                    mixed = pltpu.roll(mixed, 128 - 16 * u, 1)
            else:
                mixed = None
                for s in range(8):
                    shift = (16 * (s - (u - 8))) % 128
                    moved = pltpu.roll(wide[s][8:16], shift, 1) if shift else wide[s][8:16]
                    mixed = moved if mixed is None else jnp.where(spot == s, moved, mixed)
            lhs[32 + 8 * u : 40 + 8 * u, 128 * g : 128 * (g + 1)] = mixed

    found = None
    for d in range(D2MAX + 1):
        term = jnp.dot(lhs[8 * d : 8 * d + 128, :].astype(BF16), weights[d], preferred_element_type=F32)
        found = term if found is None else found + term
    found = found * (1.0 / math.sqrt(C))
    swap_send[...] = found[0:80]
    swap = to_core(swap_send, swap_recv, s_send, s_recv)
    out_ref[0 : 8 * SPAN, :] = found[32:128]
    out_ref[8 * SPAN : 8 * SPAN_V, :] = jnp.zeros((8 * BOXMAX, ND), F32)
    swap.wait_recv()
    taken = jnp.where(jnp.full((80, ND), sec, jnp.int32) == 0, swap_recv[...], 0.0)
    out_ref[64 : 8 * SPAN_V, :] += taken

    for group in (halves_up, halves_down, direct_up, direct_down, passed_up, passed_down):
        for copy in group:
            copy.wait_send()
    for copy in base_copies + sum(part_copies.values(), []):
        copy.wait_send()
    for copy in chan_copies:
        copy.wait_send()
    rim_copy.wait_send()
    swap.wait_send()


def search(voltages, positions, chan_delays, sub_delays):
    hbm = pl.BlockSpec(memory_space=pltpu.HBM)
    dma = pltpu.SemaphoreType.DMA
    return pl.pallas_call(
        kernel,
        out_shape=pltpu.VMEM((8 * SPAN_V, ND), F32),
        in_specs=[hbm, hbm, hbm, hbm],
        out_specs=pl.BlockSpec(memory_space=pltpu.VMEM),
        scratch_shapes=[
            pltpu.VMEM((8, 128), jnp.int32),
            pltpu.VMEM((CHANS, ND), jnp.int32),
            pltpu.VMEM((2, SPAN, 256, 256), BF16),
            pltpu.VMEM((4, CHUNKS, 512, 256), BF16),
            pltpu.VMEM((CHUNKS, 3, 512, 256), BF16),
            pltpu.VMEM((CHUNKS, 256, 256), BF16),
            pltpu.VMEM((CHUNKS, 256, 256), BF16),
            pltpu.VMEM((4, 2 * NF, 512), BF16),
            pltpu.VMEM((CHUNKS, 2 * NF, 256), F32),
            pltpu.VMEM((NF, SPAN * LOCAL), F32),
            pltpu.VMEM((NF, 128), F32),
            pltpu.VMEM((2, 512, 128), F32),
            pltpu.VMEM((2, 512, 128), F32),
            pltpu.VMEM((NK, SUBCH), jnp.int32),
            pltpu.VMEM((SUBCH, 256), F32),
            pltpu.VMEM(((SPAN + D1MAX) * LOCAL, 256), BF16),
            pltpu.VMEM((D2MAX + 1, 512, ND), BF16),
            pltpu.VMEM((4, 4, 2, 48, 128), F32),
            pltpu.VMEM((4, 4, 2, 48, 128), BF16),
            pltpu.VMEM((4, 3, 2, 48, 128), BF16),
            pltpu.VMEM((8, 4, 16, 128), BF16),
            pltpu.VMEM((CHANS, 16, 128), BF16),
            pltpu.VMEM((160, 512), F32),
            pltpu.VMEM((80, ND), F32),
            pltpu.VMEM((80, ND), F32),
            pltpu.VMEM((4, 32, 256), F32),
            dma((CHUNKS,)),
            dma,
            dma,
            dma,
            dma((6 * CHUNKS,)),
            dma((6 * CHUNKS,)),
            dma,
            dma,
            dma((2,)),
            dma((2,)),
            dma((12,)),
            dma((12,)),
            dma((CHANS,)),
            dma((CHANS,)),
            dma,
            dma,
            pltpu.SemaphoreType.REGULAR((5,)),
        ],
        compiler_params=pltpu.CompilerParams(
            collective_id=0, has_side_effects=True, vmem_limit_bytes=60 * 1024 * 1024
        ),
        name="search",
    )(
        jnp.transpose(voltages, (0, 2, 1, 3)),
        positions.reshape(8, 128),
        chan_delays,
        jnp.transpose(sub_delays),
    )


def boxcar_kernel(box_ref, ext_ref, out_ref, held, sems):
    copies = []
    for filter_index in range(NW):
        width_now = box_ref[0, filter_index]
        stride_now = box_ref[1, filter_index]
        gain = lax.rsqrt(jnp.full((8, ND), width_now, jnp.int32).astype(F32))
        summed = ext_ref[0:SPAN]
        for offset in range(1, NW + 1):
            start = jnp.minimum(offset * stride_now, BOXMAX)
            kept = jnp.where(offset < width_now, 1.0, 0.0)
            summed = summed + ext_ref[pl.ds(start, SPAN)] * kept
        held[filter_index] = summed * gain[None]
        copies.append(
            pltpu.make_async_copy(held.at[filter_index], out_ref.at[:, filter_index], sems.at[filter_index])
        )
        copies[-1].start()
    for copy in copies:
        copy.wait()


def boxcar_filter(extended, boxcars):
    filtered = pl.pallas_call(
        boxcar_kernel,
        out_shape=jax.ShapeDtypeStruct((SPAN, NW, 8, ND), F32),
        in_specs=[pl.BlockSpec(memory_space=pltpu.SMEM), pl.BlockSpec(memory_space=pltpu.VMEM)],
        out_specs=pl.BlockSpec(memory_space=pl.ANY),
        scratch_shapes=[pltpu.VMEM((NW, SPAN, 8, ND), F32), pltpu.SemaphoreType.DMA((NW,))],
        compiler_params=pltpu.CompilerParams(vmem_limit_bytes=8 * 1024 * 1024),
        name="boxcar",
    )(jnp.transpose(boxcars), extended)
    return jnp.transpose(filtered, (2, 0, 1, 3))


def per_device(voltages, positions, chan_delays, sub_delays, boxcars):
    extended = search(voltages, positions, chan_delays, sub_delays)
    return boxcar_filter(extended.reshape(SPAN_V, 8, ND), boxcars)


def solution(mesh):
    return jax.shard_map(
        per_device,
        mesh=mesh,
        in_specs=(P(None, "feed", "section", "chan"), P(), P(), P(), P()),
        out_specs=P(("chan", "feed"), "section", None, None),
        check_vma=False,
    )
```
